256 devices in a mesh: gz: 8 (over y, z_lo), ta: 32 (over z_hi, x, core).
Axes of the slice: x: 4, y: 4, z: 8 (z_hi: 4, z_lo: 2; z = z_hi * 2 + z_lo), core: 2. Of those that a mesh axis runs over, the one named last changes fastest.
Arguments:
- raw_planes: float32 [256, 2, 320, 2048], P(('gz', 'ta')), may hold values from 10 to 8000, as said below
- offsets: int32 [256, 2], replicated, may hold values from 0 to 63
Outputs:
- corrected: float32 [256, 2, 320, 2048], P(('gz', 'ta'))
- east_corr: float32 [256, 320, 256], P(('gz', 'ta'))
- south_corr: float32 [256, 256, 2048], P(('gz', 'ta'))
The draws below stay inside these ranges and needn't reach their ends.
Inputs may be any that keep to these rules, and one draw needn't show every extreme that they name: `raw_planes`: counts are positive.
All inputs are finite; a program needn't handle non-finite values.
Results may differ from the reference program's by a relative error of at most 0.0003.
Values sent between devices are 32-bit elements; how exact they have to be, the bound alone decides.
A program may use at most 128 MiB of HBM per device.

```python
import math
import jax
import jax.numpy as jnp
from jax import lax

WIDTH = 2048
INTERSECTION = 256
ROWS = 320
PLANES = 2
GRID_COLS = 8
MAX_OFFSET = 64
TILES = 256
N_TA = 32


def draw_raw_planes(key, part):
    subkeys = jax.random.split(key, 3)
    position = jnp.arange(TILES, dtype=jnp.float32) / max(TILES - 1, 1)
    levels = math.log(10.0) * position
    signal = 0.5 * jax.random.truncated_normal(subkeys[0], -3.0, 3.0, (TILES, PLANES, ROWS, WIDTH), jnp.float32)
    vignette = 0.3 * jax.random.truncated_normal(subkeys[1], -3.0, 3.0, (ROWS, WIDTH), jnp.float32)
    pedestal = 40.0 * jnp.exp(0.3 * jax.random.truncated_normal(subkeys[2], -3.0, 3.0, (ROWS, WIDTH), jnp.float32))
    return 60.0 * jnp.exp(vignette + levels[:, None, None, None] + signal) + pedestal


def place_ends(entries, rng, smallest, high):
    spot = [jax.random.randint(jax.random.fold_in(rng, axis), (), 0, length) for axis, length in enumerate(entries.shape)]
    widest = entries.shape.index(max(entries.shape))
    next_to = spot[:widest] + [(spot[widest] + 1) % entries.shape[widest]] + spot[widest + 1:]
    return entries.at[tuple(spot)].set(smallest).at[tuple(next_to)].set(high)


def setup_inputs(seed: int = 0) -> dict:
    splits = jax.random.split(jax.random.key(seed), 3)
    raw_planes = draw_raw_planes(jax.random.fold_in(splits[2], 71), 0)
    offsets = place_ends(jax.random.randint(splits[1], (TILES, 2), 0, MAX_OFFSET), jax.random.fold_in(splits[1], 1), 0, MAX_OFFSET - 1).astype(jnp.int32)
    return {"raw_planes": raw_planes, "offsets": offsets}


def correlate(own_strip, other_strip):
    rows_count, cols_count = own_strip.shape
    own_spectrum = jnp.fft.fft2(own_strip)
    other_spectrum = jnp.fft.fft2(other_strip)
    cross = own_spectrum * jnp.conj(other_spectrum)
    magnitude = jnp.abs(cross)
    weighted = cross / (magnitude + jnp.mean(magnitude) + 1e-06)
    return jnp.real(jnp.fft.ifft2(weighted)) * math.sqrt(rows_count * cols_count)

def reference(raw_planes, offsets):

    def accumulate(carry, tile_stack):
        log_planes = jnp.log(tile_stack)
        return ((carry[0] + lax.optimization_barrier(jnp.sum(log_planes, 0)), carry[1] + lax.optimization_barrier(jnp.min(log_planes, 0))), None)
    zeros_field = jnp.zeros((ROWS, WIDTH), jnp.float32)
    totals, ignored = lax.scan(accumulate, (zeros_field, zeros_field), raw_planes)
    flat_field = jnp.exp(totals[0] / (TILES * PLANES))
    dark_field = 0.5 * jnp.exp(totals[1] / TILES)
    corrected = (raw_planes - dark_field) / flat_field

    def east_strip(tile_stack, shift_cols):
        start = (WIDTH - INTERSECTION - shift_cols).astype(jnp.int32)
        mean_raw = lax.optimization_barrier(jnp.mean(lax.dynamic_slice_in_dim(tile_stack, start, INTERSECTION, 2), 0))
        dark_part = lax.dynamic_slice_in_dim(dark_field, start, INTERSECTION, 1)
        flat_part = lax.dynamic_slice_in_dim(flat_field, start, INTERSECTION, 1)
        return (mean_raw - dark_part) / flat_part

    def south_strip(tile_stack, shift_rows):
        start = (ROWS - INTERSECTION - shift_rows).astype(jnp.int32)
        mean_raw = lax.optimization_barrier(jnp.mean(lax.dynamic_slice_in_dim(tile_stack, start, INTERSECTION, 1), 0))
        dark_part = lax.dynamic_slice_in_dim(dark_field, start, INTERSECTION, 0)
        flat_part = lax.dynamic_slice_in_dim(flat_field, start, INTERSECTION, 0)
        return (mean_raw - dark_part) / flat_part
    east_all = jax.vmap(east_strip)(raw_planes, offsets[:, 0])
    south_all = jax.vmap(south_strip)(raw_planes, offsets[:, 1])
    positions = jnp.arange(TILES, dtype=jnp.int32)
    slots = positions % N_TA
    has_east = slots < N_TA - 1
    has_north = slots >= GRID_COLS
    own_west = (lax.optimization_barrier(jnp.mean(raw_planes[:, :, :, :INTERSECTION], 1)) - dark_field[:, :INTERSECTION]) / flat_field[:, :INTERSECTION]
    own_north = (lax.optimization_barrier(jnp.mean(raw_planes[:, :, :INTERSECTION, :], 1)) - dark_field[:INTERSECTION, :]) / flat_field[:INTERSECTION, :]
    east_partner = jnp.where(has_east[:, None, None], jnp.roll(own_west, -1, axis=0), 0.0)
    north_partner = jnp.where(has_north[:, None, None], jnp.roll(south_all, GRID_COLS, axis=0), 0.0)
    east_corr = lax.map(lambda paired: correlate(paired[0], paired[1]), (east_all, east_partner))
    south_corr = lax.map(lambda paired: correlate(paired[0], paired[1]), (own_north, north_partner))
    return (corrected, east_corr.astype(jnp.float32), south_corr.astype(jnp.float32))
```

```python
import math

import jax
import jax.numpy as jnp
import ml_dtypes
import numpy as np
from jax import lax
from jax.experimental import pallas as pl
from jax.experimental.pallas import tpu as pltpu
from jax.sharding import PartitionSpec as P

ROWS = 320
WIDTH = 2048
CUT = 256
GRID_COLS = 8
TILES = 256
PLANES = 2
HALF = 144
EAST_HALF = 176
MESH = pl.DeviceIdType.MESH
F32 = jnp.float32
BF16 = jnp.bfloat16


def two_parts(table):
    high = table.astype(ml_dtypes.bfloat16)
    low = (table - high.astype(np.float64)).astype(ml_dtypes.bfloat16)
    return high, low


def left_table(table):
    high, low = two_parts(table)
    return np.concatenate([high, high, low], axis=1)


def right_table(table):
    high, low = two_parts(table)
    return np.concatenate([high, high, low], axis=0)


def angles(rows, cols, length):
    product = np.outer(np.arange(rows), np.arange(cols)) % length
    return product * (2.0 * np.pi / length)


def row_tables(length, half, cols):
    count = length // 2 + 1
    turn = angles(count, length, length)
    forward = np.zeros((2 * half, length))
    forward[:count] = np.cos(turn)
    forward[half : half + count] = -np.sin(turn)
    weight = np.full((count, 1), 2.0)
    weight[0] = weight[-1] = 1.0
    scale = 1.0 / math.sqrt(length * cols)
    backward = np.zeros((length, 2 * half))
    backward[:, :count] = (weight * np.cos(turn)).T * scale
    backward[:, half : half + count] = (weight * np.sin(turn)).T * scale
    rows = np.zeros((half, 128), np.float32)
    rows[:count] = weight
    return left_table(forward), left_table(backward), rows


def south_tables():
    forward, backward, weight = row_tables(CUT, HALF, WIDTH)
    turn = angles(128, 128, 128)
    cos, sin = np.cos(turn), np.sin(turn)
    block = np.block([[cos, -sin], [sin, cos]])
    turn = angles(16, 128, WIDTH)
    twist = np.concatenate([np.cos(turn), -np.sin(turn)]).astype(np.float32)
    return forward, backward, weight, right_table(block), twist


def east_tables():
    forward, backward, weight = row_tables(ROWS, EAST_HALF, CUT)
    turn = angles(CUT, CUT, CUT)
    both = np.concatenate([np.cos(turn), np.sin(turn)], axis=1)
    return forward, backward, weight, right_table(both)


def dot(a, b):
    return jnp.dot(a, b, preferred_element_type=F32)


def three(x, axis):
    high = x.astype(BF16)
    low = (x - high.astype(F32)).astype(BF16)
    return jnp.concatenate([high, low, high], axis=axis)


def butterfly(re, im):
    size = len(re)
    if size == 1:
        return re, im
    even_re, even_im = butterfly(re[::2], im[::2])
    odd_re, odd_im = butterfly(re[1::2], im[1::2])
    top_re, top_im, low_re, low_im = [], [], [], []
    root = math.sqrt(0.5)
    for k in range(size // 2):
        a, b = odd_re[k], odd_im[k]
        if k == 0:
            pass
        elif 4 * k == size:
            a, b = b, -a
        elif 8 * k == size:
            a, b = root * (a + b), root * (b - a)
        elif 8 * k == 3 * size:
            a, b = root * (b - a), -root * (a + b)
        else:
            c, s = math.cos(2 * math.pi * k / size), math.sin(2 * math.pi * k / size)
            a, b = c * a + s * b, c * b - s * a
        top_re.append(even_re[k] + a)
        top_im.append(even_im[k] + b)
        low_re.append(even_re[k] - a)
        low_im.append(even_im[k] - b)
    return top_re + low_re, top_im + low_im


def at(start, size, step):
    return pl.ds(pl.multiple_of(start, step), size)


def loop(count, f):
    lax.fori_loop(0, count, lambda i, c: (f(i), c)[1], 0)


def south_forward(strip, dark, inv, rows3, cols3, twist, y, z, spec):
    def rows_step(i):
        cols = at(i * 256, 256, 256)
        x = (strip[:, cols] - dark[:, cols]) * inv[:, cols]
        y[:, cols] = dot(rows3[...], three(x, 0))

    loop(8, rows_step)

    def turn_step(i):
        top, low = at(i * 8, 8, 8), at(HALF + i * 8, 8, 8)
        re = [y[top, 128 * a : 128 * a + 128] for a in range(16)]
        im = [y[low, 128 * a : 128 * a + 128] for a in range(16)]
        re, im = butterfly(re, im)
        for k in range(16):
            c, s = twist[k : k + 1, :], twist[16 + k : 17 + k, :]
            to = at(k * HALF + i * 8, 8, 8)
            z[to, :128] = re[k] * c - im[k] * s
            z[to, 128:] = re[k] * s + im[k] * c

    loop(HALF // 8, turn_step)

    def cols_step(i):
        to = at(i * 576, 576, 8)
        spec[to, :] = dot(three(z[to, :], 1), cols3[...])

    loop(4, cols_step)


def own_kernel(strip, dark, inv, rows3, cols3, twist, spec, y, z):
    south_forward(strip, dark, inv, rows3, cols3, twist, y, z, spec)


def south_kernel(own, strip, dark, inv, rows3, back3, weight, cols3, twist, out, y, z, spec, mag):
    south_forward(strip, dark, inv, rows3, cols3, twist, y, z, spec)

    def cross_step(i, total):
        part = jnp.zeros((8, 128), F32)
        for k in range(16):
            here = at(k * HALF + i * 8, 8, 8)
            ar, ai = own[here, :128], own[here, 128:]
            br, bi = spec[here, :128], spec[here, 128:]
            cr = ar * br + ai * bi
            ci = ai * br - ar * bi
            size = jnp.sqrt(cr * cr + ci * ci)
            z[here, :128] = cr
            z[here, 128:] = -ci
            mag[here, :] = size
            part = part + size
        return total + part * weight[at(i * 8, 8, 8), :]

    total = lax.fori_loop(0, HALF // 8, cross_step, jnp.zeros((8, 128), F32))
    floor = jnp.sum(total) * (1.0 / (CUT * WIDTH)) + 1e-06

    def cols_step(i):
        here = at(i * 288, 288, 8)
        scale = 1.0 / (mag[here, :] + floor)
        x = jnp.concatenate([z[here, :128] * scale, z[here, 128:] * scale], axis=1)
        spec[here, :] = dot(three(x, 1), cols3[...])

    loop(8, cols_step)

    def turn_step(i):
        re, im = [], []
        for k in range(16):
            c, s = twist[k : k + 1, :], twist[16 + k : 17 + k, :]
            here = at(k * HALF + i * 8, 8, 8)
            a, b = spec[here, :128], spec[here, 128:]
            re.append(a * c - b * s)
            im.append(a * s + b * c)
        re, im = butterfly(re, im)
        top, low = at(i * 8, 8, 8), at(HALF + i * 8, 8, 8)
        for a in range(16):
            y[top, 128 * a : 128 * a + 128] = re[a]
            y[low, 128 * a : 128 * a + 128] = im[a]

    loop(HALF // 8, turn_step)

    def rows_step(i):
        cols = at(i * 256, 256, 256)
        out[:, cols] = dot(back3[...], three(y[:, cols], 0))

    loop(8, rows_step)


def east_kernel(own, other, dark, inv, dark2, inv2, rows3, back3, weight, cols3, out):
    half = EAST_HALF
    x = jnp.concatenate([(own[...] - dark[...]) * inv[...], (other[...] - dark2[...]) * inv2[...]], axis=1)
    y = dot(rows3[...], three(x, 0))

    def columns(v):
        p = dot(three(v, 1), cols3[...])
        return p[:half, :CUT] + p[half:, CUT:], p[half:, :CUT] - p[:half, CUT:]

    ar, ai = columns(y[:, :CUT])
    br, bi = columns(y[:, CUT:])
    cr = ar * br + ai * bi
    ci = ai * br - ar * bi
    size = jnp.sqrt(cr * cr + ci * ci)
    weighted = (size[:, :128] + size[:, 128:]) * weight[...]
    floor = jnp.sum(weighted) * (1.0 / (ROWS * CUT)) + 1e-06
    scale = 1.0 / (size + floor)
    vr, vi = columns(jnp.concatenate([cr * scale, -ci * scale], axis=0))
    out[...] = dot(back3[...], three(jnp.concatenate([vr, vi], axis=0), 0))


def log_kernel(raw, out):
    first, second = jnp.log(raw[0]), jnp.log(raw[1])
    out[0] = first + second
    out[1] = jnp.minimum(first, second)


def logs_of(tile):
    rows = 32
    return pl.pallas_call(
        log_kernel,
        grid=(ROWS // rows,),
        in_specs=[pl.BlockSpec((PLANES, rows, WIDTH), lambda i: (0, i, 0))],
        out_specs=pl.BlockSpec((2, rows, WIDTH), lambda i: (0, i, 0)),
        out_shape=jax.ShapeDtypeStruct((2, ROWS, WIDTH), F32),
        cost_estimate=pl.CostEstimate(flops=4 * ROWS * WIDTH, bytes_accessed=16 * ROWS * WIDTH, transcendentals=2 * ROWS * WIDTH),
        name="logs",
    )(tile)


SIDE = ROWS // 2


def field_kernel(logs, out, acc, first, recv1, recv2, recv3, recv4, recv_z, recv_a, recv_b, send, recv):
    gz, ta = lax.axis_index("gz"), lax.axis_index("ta")
    y, z_lo = gz // 2, gz % 2
    z_hi, x, core = ta // 8, (ta // 2) % 4, ta % 2

    def device(x, y, z_hi, z_lo, core):
        return (y * 2 + z_lo, z_hi * 8 + x * 2 + core)

    def beside(p):
        return p + 1 - 2 * (p % 2)

    def across(p):
        return 3 - p

    def gray(p):
        return (p + p // 2) % 2

    other = 1 - core

    def along(axis, move):
        on_x = (1 - core) if axis == 0 else core
        return device(x + on_x * (move(x) - x), y + (1 - on_x) * (move(y) - y), z_hi, z_lo, core)

    place = (x + core * (y - x), y + core * (x - y))
    partner_core = device(x, y, z_hi, z_lo, other)
    partner = {(axis, move): along(axis, move) for axis in (0, 1) for move in (beside, across)}
    partner_lo = device(x, y, z_hi, 1 - z_lo, core)
    partner_a = device(x, y, beside(z_hi), z_lo, core)
    partner_b = device(x, y, across(z_hi), z_lo, core)

    barrier = pltpu.get_barrier_semaphore()
    everyone = [partner_core, *partner.values(), partner_lo, partner_a, partner_b]
    for d in everyone:
        pl.semaphore_signal(barrier, inc=1, device_id=d, device_id_type=MESH)
    pl.semaphore_wait(barrier, len(everyone))

    count = [0]
    started = []

    def copy(src, dst, to):
        i = count[0]
        count[0] += 1
        c = pltpu.make_async_remote_copy(
            src_ref=src, dst_ref=dst, send_sem=send.at[i], recv_sem=recv.at[i], device_id=to, device_id_type=MESH
        )
        c.start()
        started.append(c)
        return c

    def rows(k):
        return pl.ds(k * SIDE, SIDE)

    flight = [copy(logs.at[other, rows(k)], first.at[rows(k)], partner_core) for k in (0, 1)]
    moves = [
        [(0, beside, gray), (0, across, lambda p: p // 2), (1, beside, gray), (1, across, lambda p: p // 2)],
        [(0, across, lambda p: p // 2), (0, beside, gray), (1, across, lambda p: p // 2), (1, beside, gray)],
    ]
    into = [recv1, recv2, recv3, recv4]
    widths = [1024, 512, 256, 128]
    bases = [[0], [0]]
    bits = [[], []]
    for step in range(5):
        for k in (0, 1):
            flight[k].wait_recv()
            if step == 0:

                def add_first(i, k=k):
                    r = at(k * SIDE + i * 8, 8, 8)
                    acc[r, :] = logs[core, r, :] + first[r, :]

                loop(SIDE // 8, add_first)
            else:
                w = widths[step - 1]
                base = bases[k][step]
                buf = into[step - 1]

                def add_next(i, k=k, w=w, base=base, buf=buf):
                    r = at(k * SIDE + i * 8, 8, 8)
                    c = at(base, w, 128)
                    acc[r, c] = acc[r, c] + buf[k, at(i * 8, 8, 8), :]

                loop(SIDE // 8, add_next)
            if step < 4:
                axis, move, bit = moves[k][step]
                w = widths[step]
                b = bit(place[axis])
                base = bases[k][step]
                flight[k] = copy(
                    acc.at[rows(k), at(base + (1 - b) * w, w, 128)], into[step].at[k], partner[(axis, move)]
                )
                bases[k].append(base + b * w)
                bits[k].append(b)

    col_a, col_b = bases[0][4], bases[1][4]
    mine = col_a + z_lo * (col_b - col_a)
    theirs = col_b + z_lo * (col_a - col_b)
    col = at(mine, 128, 128)
    top = z_lo * SIDE
    f = copy(acc.at[at((1 - z_lo) * SIDE, SIDE, 8), at(theirs, 128, 128)], recv_z, partner_lo)
    f.wait_recv()
    acc[at(top, SIDE, 8), col] += recv_z[...]
    g, h = gray(z_hi), z_hi // 2
    f = copy(acc.at[at(top + (1 - g) * 80, 80, 8), col], recv_a, partner_a)
    top_a = top + g * 80
    f.wait_recv()
    acc[at(top_a, 80, 8), col] += recv_a[...]
    f = copy(acc.at[at(top_a + (1 - h) * 40, 40, 8), col], recv_b, partner_b)
    top_b = top_a + h * 40
    f.wait_recv()
    total = acc[at(top_b, 40, 8), col] + recv_b[...]
    is_floor = core.astype(F32)
    scale = is_floor * (1.0 / TILES) - (1.0 - is_floor) * (1.0 / (TILES * PLANES))
    out[core, at(top_b, 40, 8), col] = (1.0 - 0.5 * is_floor) * jnp.exp(total * scale)

    def give(r, c, to):
        return copy(out.at[core, r, c], out.at[core, r, c], to)

    give(at(top_b, 40, 8), col, partner_b).wait_recv()
    give(at(top_a, 80, 8), col, partner_a).wait_recv()
    give(at(top, SIDE, 8), col, partner_lo).wait_recv()
    for step in (3, 2, 1, 0):
        for k in (0, 1):
            if step < 3:
                flight[k].wait_recv()
            axis, move, _ = moves[k][step]
            w = widths[step]
            flight[k] = give(rows(k), at(bases[k][step + 1], w, 128), partner[(axis, move)])
    for k in (0, 1):
        flight[k].wait_recv()
        flight[k] = copy(out.at[core, rows(k)], out.at[core, rows(k)], partner_core)
    for k in (0, 1):
        flight[k].wait_recv()
    for c in started:
        c.wait_send()


COPIES = 2 + 8 + 3 + 3 + 8 + 2


def fields_of(logs):
    return pl.pallas_call(
        field_kernel,
        out_shape=jax.ShapeDtypeStruct((2, ROWS, WIDTH), F32),
        in_specs=[pl.BlockSpec(memory_space=pltpu.VMEM)],
        out_specs=pl.BlockSpec(memory_space=pltpu.VMEM),
        scratch_shapes=[
            pltpu.VMEM((ROWS, WIDTH), F32),
            pltpu.VMEM((ROWS, WIDTH), F32),
            pltpu.VMEM((2, SIDE, 1024), F32),
            pltpu.VMEM((2, SIDE, 512), F32),
            pltpu.VMEM((2, SIDE, 256), F32),
            pltpu.VMEM((2, SIDE, 128), F32),
            pltpu.VMEM((SIDE, 128), F32),
            pltpu.VMEM((80, 128), F32),
            pltpu.VMEM((40, 128), F32),
            pltpu.SemaphoreType.DMA((COPIES,)),
            pltpu.SemaphoreType.DMA((COPIES,)),
        ],
        compiler_params=pltpu.CompilerParams(collective_id=0, has_side_effects=True, vmem_limit_bytes=30 << 20),
        cost_estimate=pl.CostEstimate(flops=8 * ROWS * WIDTH, bytes_accessed=100 << 20, transcendentals=40 * 128),
        name="fields",
    )(logs)


def plain_call(kernel, out, scratch, flops, args, name):
    return pl.pallas_call(
        kernel,
        out_shape=jax.ShapeDtypeStruct(out, F32),
        scratch_shapes=[pltpu.VMEM(s, F32) for s in scratch],
        compiler_params=pltpu.CompilerParams(vmem_limit_bytes=40 << 20),
        cost_estimate=pl.CostEstimate(flops=flops, bytes_accessed=8 << 20, transcendentals=0),
        name=name,
    )(*args)


def shifted(value, steps, count):
    first, last = (max(0, -steps), min(count, count - steps))
    return lax.ppermute(value, "ta", [(source, source + steps) for source in range(first, last)])


def body(raw_planes, offsets):
    tile = raw_planes[0]
    count = lax.axis_size("ta")
    slot = lax.axis_index("ta")
    own_tile = lax.axis_index("gz") * count + slot
    has_east = slot < count - 1
    has_north = slot >= GRID_COLS
    own_east = offsets[own_tile, 0]
    own_south = offsets[own_tile, 1]
    north_south = offsets[jnp.maximum(own_tile - GRID_COLS, 0), 1]

    south_mean = jnp.mean(lax.dynamic_slice_in_dim(tile, ROWS - CUT - own_south, CUT, 1), 0)
    south_in = shifted(south_mean, GRID_COLS, count)
    west_in = shifted(jnp.mean(tile[:, :, :CUT], 0), -1, count)

    fields = fields_of(logs_of(tile))
    inv, dark = fields[0], fields[1]
    corrected = (tile - dark) * inv

    east_start = WIDTH - CUT - own_east
    east_mean = jnp.mean(lax.dynamic_slice_in_dim(tile, east_start, CUT, 2), 0)
    east_dark = lax.dynamic_slice_in_dim(dark, east_start, CUT, 1)
    east_inv = lax.dynamic_slice_in_dim(inv, east_start, CUT, 1)
    west_inv = jnp.where(has_east, inv[:, :CUT], 0.0)
    forward, backward, weight, cols3 = east_tables()
    east_corr = plain_call(
        east_kernel,
        (ROWS, CUT),
        [],
        10**9,
        (east_mean, west_in, east_dark, east_inv, dark[:, :CUT], west_inv, forward, backward, weight, cols3),
        "east",
    )

    forward, backward, weight, cols3, twist = south_tables()
    north_mean = jnp.mean(tile[:, :CUT], 0)
    own_spec = plain_call(
        own_kernel,
        (16 * HALF, 256),
        [(2 * HALF, WIDTH), (16 * HALF, 256)],
        2 * 10**9,
        (north_mean, dark[:CUT], inv[:CUT], forward, cols3, twist),
        "own",
    )
    start = ROWS - CUT - north_south
    south_dark = lax.dynamic_slice_in_dim(dark, start, CUT, 0)
    south_inv = jnp.where(has_north, lax.dynamic_slice_in_dim(inv, start, CUT, 0), 0.0)
    south_corr = plain_call(
        south_kernel,
        (CUT, WIDTH),
        [(2 * HALF, WIDTH), (16 * HALF, 256), (16 * HALF, 256), (16 * HALF, 128)],
        4 * 10**9,
        (own_spec, south_in, south_dark, south_inv, forward, backward, weight, cols3, twist),
        "south",
    )
    return (corrected[None], east_corr[None], south_corr[None])


def solution(mesh):
    in_specs = (P(("gz", "ta"), None, None, None), P())
    out_specs = (
        P(("gz", "ta"), None, None, None),
        P(("gz", "ta"), None, None),
        P(("gz", "ta"), None, None),
    )
    return jax.shard_map(body, mesh=mesh, in_specs=in_specs, out_specs=out_specs, check_vma=False)
```

```python
import math

import jax
import jax.numpy as jnp
import ml_dtypes
import numpy as np
from jax import lax
from jax.experimental import pallas as pl
from jax.experimental.pallas import tpu as pltpu
from jax.sharding import PartitionSpec as P

ROWS = 320
WIDTH = 2048
CUT = 256
GRID_COLS = 8
TILES = 256
PLANES = 2
HALF = 144
EAST_HALF = 176
MESH = pl.DeviceIdType.MESH
F32 = jnp.float32
BF16 = jnp.bfloat16


def two_parts(table):
    high = table.astype(ml_dtypes.bfloat16)
    low = (table - high.astype(np.float64)).astype(ml_dtypes.bfloat16)
    return high, low


def stacked(table):
    return np.stack(two_parts(table))


def left_table(table):
    high, low = two_parts(table)
    return np.concatenate([high, high, low], axis=1)


def right_table(table):
    high, low = two_parts(table)
    return np.concatenate([high, high, low], axis=0)


def angles(rows, cols, length):
    product = np.outer(np.arange(rows), np.arange(cols)) % length
    return product * (2.0 * np.pi / length)


def row_tables(length, half, cols, left_table):
    count = length // 2 + 1
    turn = angles(count, length, length)
    forward = np.zeros((2 * half, length))
    forward[:count] = np.cos(turn)
    forward[half : half + count] = -np.sin(turn)
    weight = np.full((count, 1), 2.0)
    weight[0] = weight[-1] = 1.0
    scale = 1.0 / math.sqrt(length * cols)
    backward = np.zeros((length, 2 * half))
    backward[:, :count] = (weight * np.cos(turn)).T * scale
    backward[:, half : half + count] = (weight * np.sin(turn)).T * scale
    rows = np.zeros((half, 128), np.float32)
    rows[:count] = weight
    return left_table(forward), left_table(backward), rows


def south_tables():
    forward, backward, weight = row_tables(CUT, HALF, WIDTH, left_table)
    turn = angles(128, 128, 128)
    cos, sin = np.cos(turn), np.sin(turn)
    block = np.block([[cos, -sin], [sin, cos]])
    turn = angles(16, 128, WIDTH)
    twist = np.concatenate([np.cos(turn), -np.sin(turn)]).astype(np.float32)
    return forward, backward, weight, right_table(block), twist


def east_tables():
    forward, backward, weight = row_tables(ROWS, EAST_HALF, CUT, stacked)
    turn = angles(CUT, CUT, CUT)
    both = np.concatenate([np.cos(turn), np.sin(turn)], axis=1)
    return forward, backward, weight, stacked(both)


def dot(a, b):
    return jnp.dot(a, b, preferred_element_type=F32)


def three(x, axis):
    high, low = split(x)
    return jnp.concatenate([high, low, high], axis=axis)


def split(x):
    high = x.astype(BF16)
    return high, (x - high.astype(F32)).astype(BF16)


def left_dot(table, x):
    high, low = split(x)
    return dot(table[0], high) + (dot(table[0], low) + dot(table[1], high))


def right_dot(x, table):
    high, low = split(x)
    return dot(high, table[0]) + (dot(low, table[0]) + dot(high, table[1]))


def butterfly(re, im):
    size = len(re)
    if size == 1:
        return re, im
    even_re, even_im = butterfly(re[::2], im[::2])
    odd_re, odd_im = butterfly(re[1::2], im[1::2])
    top_re, top_im, low_re, low_im = [], [], [], []
    root = math.sqrt(0.5)
    for k in range(size // 2):
        a, b = odd_re[k], odd_im[k]
        if k == 0:
            pass
        elif 4 * k == size:
            a, b = b, -a
        elif 8 * k == size:
            a, b = root * (a + b), root * (b - a)
        elif 8 * k == 3 * size:
            a, b = root * (b - a), -root * (a + b)
        else:
            c, s = math.cos(2 * math.pi * k / size), math.sin(2 * math.pi * k / size)
            a, b = c * a + s * b, c * b - s * a
        top_re.append(even_re[k] + a)
        top_im.append(even_im[k] + b)
        low_re.append(even_re[k] - a)
        low_im.append(even_im[k] - b)
    return top_re + low_re, top_im + low_im


def at(start, size, step):
    return pl.ds(pl.multiple_of(start, step), size)


def loop(count, f):
    lax.fori_loop(0, count, lambda i, c: (f(i), c)[1], 0)


def moved(x, steps, axis):
    count = jnp.full(x.shape, steps, jnp.int32)
    for bit in (32, 16, 8, 4, 2, 1):
        x = jnp.where((count & bit) != 0, pltpu.roll(x, bit, axis), x)
    return x


def aligned(start):
    base = jnp.minimum(start // 8 * 8, ROWS - CUT - 8)
    return base, (16 - (start - base)) % 16


def south_forward(strip_of, rows3, cols3, twist, y, z, spec):
    def rows_step(i):
        cols = at(i * 256, 256, 256)
        y[:, cols] = dot(rows3[...], three(strip_of(cols), 0))

    loop(8, rows_step)

    def turn_step(i):
        top, low = at(i * 8, 8, 8), at(HALF + i * 8, 8, 8)
        re = [y[top, 128 * a : 128 * a + 128] for a in range(16)]
        im = [y[low, 128 * a : 128 * a + 128] for a in range(16)]
        re, im = butterfly(re, im)
        for k in range(16):
            c, s = twist[k : k + 1, :], twist[16 + k : 17 + k, :]
            to = at(k * HALF + i * 8, 8, 8)
            z[to, :128] = re[k] * c - im[k] * s
            z[to, 128:] = re[k] * s + im[k] * c

    loop(HALF // 8, turn_step)

    def cols_step(i):
        to = at(i * 576, 576, 8)
        spec[to, :] = dot(three(z[to, :], 1), cols3[...])

    loop(4, cols_step)


def south_kernel(
    offsets, own, tile, fields, strip, east, rows3, back3, weight, cols3, twist,
    corrected, east_out, out, y, z, spec, mag, ready, inv, dark, sems,
):
    slot = lax.axis_index("ta")
    north = jnp.maximum(lax.axis_index("gz") * lax.axis_size("ta") + slot - GRID_COLS, 0)
    start = ROWS - CUT - offsets[north, 1]
    has_north = (slot >= GRID_COLS).astype(F32)

    def correct(i):
        r = at(i * 8, 8, 8)
        for c in range(0, WIDTH, 512):
            cols = slice(c, c + 512)
            g, d = fields[0, r, cols], fields[1, r, cols]
            for p in range(PLANES):
                ready[p, r, cols] = (tile[p, r, cols] - d) * g

    loop(ROWS // 8, correct)
    writes = [pltpu.make_async_copy(ready, corrected, sems.at[0]), pltpu.make_async_copy(east, east_out, sems.at[1])]
    for w in writes:
        w.start()

    base, turn = aligned(start)

    def cut(i):
        for c in range(0, WIDTH, 512):
            cols = slice(c, c + 512)
            window = at(base + i * 8, 16, 8)
            inv[at(i * 8, 8, 8), cols] = pltpu.roll(fields[0, window, cols], turn, 0)[:8] * has_north
            dark[at(i * 8, 8, 8), cols] = pltpu.roll(fields[1, window, cols], turn, 0)[:8]

    loop(CUT // 8, cut)

    def strip_of(cols):
        return (0.5 * strip[:, cols] - dark[:, cols]) * inv[:, cols]

    south_forward(strip_of, rows3, cols3, twist, y, z, spec)

    def cross_step(i, total):
        part = jnp.zeros((8, 128), F32)
        for k in range(16):
            here = at(k * HALF + i * 8, 8, 8)
            ar, ai = own[here, :128], own[here, 128:]
            br, bi = spec[here, :128], spec[here, 128:]
            cr = ar * br + ai * bi
            ci = ai * br - ar * bi
            size = jnp.sqrt(cr * cr + ci * ci)
            z[here, :128] = cr
            z[here, 128:] = -ci
            mag[here, :] = size
            part = part + size
        return total + part * weight[at(i * 8, 8, 8), :]

    total = lax.fori_loop(0, HALF // 8, cross_step, jnp.zeros((8, 128), F32))
    floor = jnp.sum(total) * (1.0 / (CUT * WIDTH)) + 1e-06

    def cols_step(i):
        here = at(i * 288, 288, 8)
        scale = 1.0 / (mag[here, :] + floor)
        x = jnp.concatenate([z[here, :128] * scale, z[here, 128:] * scale], axis=1)
        spec[here, :] = dot(three(x, 1), cols3[...])

    loop(8, cols_step)

    def turn_step(i):
        re, im = [], []
        for k in range(16):
            c, s = twist[k : k + 1, :], twist[16 + k : 17 + k, :]
            here = at(k * HALF + i * 8, 8, 8)
            a, b = spec[here, :128], spec[here, 128:]
            re.append(a * c - b * s)
            im.append(a * s + b * c)
        re, im = butterfly(re, im)
        top, low = at(i * 8, 8, 8), at(HALF + i * 8, 8, 8)
        for a in range(16):
            y[top, 128 * a : 128 * a + 128] = re[a]
            y[low, 128 * a : 128 * a + 128] = im[a]

    loop(HALF // 8, turn_step)

    def rows_step(i):
        cols = at(i * 256, 256, 256)
        out[:, cols] = dot(back3[...], three(y[:, cols], 0))

    loop(8, rows_step)
    for w in writes:
        w.wait()


def east_into(out, x, rows3, back3, weight, cols3):
    half = EAST_HALF
    y = left_dot(rows3, x)

    def columns(v):
        p = right_dot(v, cols3)
        return p[:half, :CUT] + p[half:, CUT:], p[half:, :CUT] - p[:half, CUT:]

    ar, ai = columns(y[:, :CUT])
    br, bi = columns(y[:, CUT:])
    cr = ar * br + ai * bi
    ci = ai * br - ar * bi
    size = jnp.sqrt(cr * cr + ci * ci)
    weighted = (size[:, :128] + size[:, 128:]) * weight[...]
    floor = jnp.sum(weighted) * (1.0 / (ROWS * CUT)) + 1e-06
    scale = 1.0 / (size + floor)
    vr, vi = columns(jnp.concatenate([cr * scale, -ci * scale], axis=0))
    out[...] = left_dot(back3, jnp.concatenate([vr, vi], axis=0))


CHAINS = 4
BAND = ROWS // CHAINS
RING = 8
BLOCK = ROWS // RING
WIDTHS = (1024, 512, 256, 128)
REACH = 3


def first_kernel(
    offsets, raw, *refs,
):
    tables_hbm, refs = refs[:7], refs[7:]
    tables, refs = refs[-9:-2], (*refs[:-9], *refs[-2:])
    (
        out, tile, strip, spec, east,
        sums, west, mine, logs, acc, first, recv1, recv2, recv3, recv4, near, far, hop, spec_y, spec_z, both, load, send, recv,
    ) = refs
    rows3, cols3, twist, rows3_e, back3_e, weight_e, cols3_e = tables
    gz, ta = lax.axis_index("gz"), lax.axis_index("ta")
    y, z = gz // 2, (ta // 8) * 2 + gz % 2
    x, core = (ta // 2) % 4, ta % 2
    other = 1 - core

    loads = []
    for q in range(CHAINS):
        band = pl.ds(q * BAND, BAND)
        c = pltpu.make_async_copy(raw.at[:, band], tile.at[:, band], load.at[q])
        c.start()
        loads.append(c)

    table_loads = []
    for i, (src, dst) in enumerate(zip(tables_hbm, tables)):
        c = pltpu.make_async_copy(src, dst, load.at[CHAINS + i])
        c.start()
        table_loads.append(c)

    def device(x, y, z, core):
        z = (z + RING) % RING
        return (y * 2 + z % 2, (z // 2) * 8 + x * 2 + core)

    def beside(p):
        return p + 1 - 2 * (p % 2)

    def across(p):
        return 3 - p

    def gray(p):
        return (p + p // 2) % 2

    def upper(p):
        return p // 2

    def along(axis, move):
        on_x = (1 - core) if axis == 0 else core
        return device(x + on_x * (move(x) - x), y + (1 - on_x) * (move(y) - y), z, core)

    place = (x + core * (y - x), y + core * (x - y))
    partner_core = device(x, y, z, other)
    partner = {(axis, move): along(axis, move) for axis in (0, 1) for move in (beside, across)}
    down = [device(x, y, z - d, core) for d in range(1, REACH + 1)]
    up = [device(x, y, z + d, core) for d in range(1, REACH + 1)]
    count_ta = lax.axis_size("ta")
    before, after = (gz, (ta + count_ta - 1) % count_ta), (gz, (ta + 1) % count_ta)

    south = (gz, (ta + GRID_COLS) % count_ta)
    north = (gz, (ta + count_ta - GRID_COLS) % count_ta)
    has_south, has_north = ta < count_ta - GRID_COLS, ta >= GRID_COLS
    own_tile = gz * count_ta + ta

    barrier = pltpu.get_barrier_semaphore()
    everyone = [partner_core, *partner.values(), *down, *up, before, after, south, north]
    for d in everyone:
        pl.semaphore_signal(barrier, inc=1, device_id=d, device_id_type=MESH)

    count = [0]
    started = []

    def copy(src, dst, to):
        i = count[0]
        count[0] += 1
        c = pltpu.make_async_remote_copy(
            src_ref=src, dst_ref=dst, send_sem=send.at[i], recv_sem=recv.at[i], device_id=to, device_id_type=MESH
        )
        c.start()
        started.append(c)
        return c

    def band(q):
        return pl.ds(q * BAND, BAND)

    for q in range(CHAINS):
        loads[q].wait()

        def add_planes(i, q=q):
            r = at(q * BAND + i * 8, 8, 8)
            sums[r, :] = tile[0, r, :] + tile[1, r, :]

        loop(BAND // 8, add_planes)

    def cut(i):
        cols = at(i * 128, 128, 128)
        mine[:, cols] = moved(sums[:, cols], offsets[own_tile, 1], 0)[ROWS - CUT :]

    loop(WIDTH // 128, cut)
    pl.semaphore_wait(barrier, len(everyone))
    south_copy = pltpu.make_async_remote_copy(
        src_ref=mine, dst_ref=strip, send_sem=send.at[COPIES], recv_sem=recv.at[COPIES], device_id=south, device_id_type=MESH
    )

    @pl.when(has_south)
    def _():
        south_copy.start()

    @pl.when(jnp.logical_not(has_north))
    def _():
        strip[...] = jnp.zeros_like(strip)

    beside_copy = copy(sums.at[:, pl.ds(0, CUT)], west, before)

    flight = []
    for q in range(CHAINS):

        def take(i, q=q):
            r = at(q * BAND + i * 8, 8, 8)
            for c in range(0, WIDTH, 512):
                cols = slice(c, c + 512)
                one, two = jnp.log(tile[0, r, cols]), jnp.log(tile[1, r, cols])
                logs[0, r, cols] = one + two
                logs[1, r, cols] = jnp.minimum(one, two)

        loop(BAND // 8, take)
        flight.append(copy(logs.at[other, band(q)], first.at[band(q)], partner_core))

    orders = [
        [(0, beside, gray), (0, across, upper), (1, beside, gray), (1, across, upper)],
        [(0, across, upper), (0, beside, gray), (1, across, upper), (1, beside, gray)],
    ]
    moves = [orders[q % 2] for q in range(CHAINS)]
    into = [recv1, recv2, recv3, recv4]
    bases = [[0] for q in range(CHAINS)]
    steps = len(WIDTHS)
    for step in range(steps + 1):
        for q in range(CHAINS):
            flight[q].wait_recv()
            if step == 0:

                def add_first(i, q=q):
                    r = at(q * BAND + i * 8, 8, 8)
                    acc[r, :] = logs[core, r, :] + first[r, :]

                loop(BAND // 8, add_first)
            else:
                w = WIDTHS[step - 1]

                def add_next(i, q=q, c=at(bases[q][step], w, 128), buf=into[step - 1]):
                    r = at(q * BAND + i * 8, 8, 8)
                    acc[r, c] = acc[r, c] + buf[r, :]

                loop(BAND // 8, add_next)
            if step < steps:
                axis, move, bit = moves[q][step]
                w = WIDTHS[step]
                b = bit(place[axis])
                base = bases[q][step]
                flight[q] = copy(
                    acc.at[band(q), at(base + (1 - b) * w, w, 128)], into[step].at[band(q)], partner[(axis, move)]
                )
                bases[q].append(base + b * w)

    def block(shift):
        j = (z + shift + RING) % RING
        col = bases[0][steps] + ((j // 2) % 2) * (bases[1][steps] - bases[0][steps])
        return at(j * BLOCK, BLOCK, 8), at(col, 128, 128)

    fars, nears = [], []
    for d in range(1, REACH + 1):
        r, c = block(4 - d)
        fars.append(copy(acc.at[r, c], far.at[d - 1], down[d - 1]))
    for d in range(1, REACH + 1):
        r, c = block(-d)
        nears.append(copy(acc.at[r, c], near.at[d - 1], down[d - 1]))
    for f in fars:
        f.wait_recv()
    r, c = block(4)
    acc[r, c] = (acc[r, c] + far[0]) + (far[1] + far[2])
    f = copy(acc.at[r, c], hop.at[0], down[2])
    f.wait_recv()
    f = copy(hop.at[0], hop.at[1], down[0])
    for n in nears:
        n.wait_recv()
    r, c = block(0)
    total = (acc[r, c] + near[0]) + (near[1] + near[2])
    f.wait_recv()
    total = total + hop[1]
    is_floor = core.astype(F32)
    scale = is_floor * (1.0 / TILES) - (1.0 - is_floor) * (1.0 / (TILES * PLANES))
    out[core, r, c] = (1.0 - 0.5 * is_floor) * jnp.exp(total * scale)

    def give(r, c, to):
        return copy(out.at[core, r, c], out.at[core, r, c], to)

    ones = [give(*block(0), to) for to in down]
    ones[0].wait_recv()
    f = give(*block(1), down[2])
    f.wait_recv()
    fours = [give(*block(4), to) for to in down]
    for f in ones[1:] + fours:
        f.wait_recv()
    for step in range(steps - 1, -1, -1):
        for q in range(CHAINS):
            if step < steps - 1:
                flight[q].wait_recv()
            axis, move, _ = moves[q][step]
            flight[q] = give(band(q), at(bases[q][step + 1], WIDTHS[step], 128), partner[(axis, move)])
    for q in range(CHAINS):
        flight[q].wait_recv()
        flight[q] = give(band(q), slice(None), partner_core)
    for q in range(CHAINS):
        flight[q].wait_recv()
    beside_copy.wait_recv()

    for c in table_loads:
        c.wait()

    def own_of(cols):
        return (0.5 * sums[:CUT, cols] - out[1, :CUT, cols]) * out[0, :CUT, cols]

    south_forward(own_of, rows3, cols3, twist, spec_y, spec_z, spec)
    has_east = (ta < count_ta - 1).astype(F32)

    def strips(i):
        r, last = at(i * 64, 64, 64), slice(WIDTH - 3 * 128, WIDTH)
        eastern = (0.5 * sums[r, last] - out[1, r, last]) * out[0, r, last]
        both[r, :CUT] = moved(eastern, offsets[own_tile, 0], 1)[:, 128:]
        both[r, CUT:] = (0.5 * west[r, :] - out[1, r, :CUT]) * out[0, r, :CUT] * has_east

    loop(ROWS // 64, strips)
    east_into(east, both[...], rows3_e, back3_e, weight_e, cols3_e)

    @pl.when(has_north)
    def _():
        south_copy.wait_recv()

    for c in started:
        c.wait_send()

    @pl.when(has_south)
    def _():
        south_copy.wait_send()


COPIES = CHAINS * 2 * (1 + len(WIDTHS)) + 1 + (2 * REACH + 2) + (2 * REACH + 1)


VMEM = pl.BlockSpec(memory_space=pltpu.VMEM)
SMEM = pl.BlockSpec(memory_space=pltpu.SMEM)
ANY = pl.BlockSpec(memory_space=pl.ANY)
HBM = pl.BlockSpec(memory_space=pltpu.HBM)
SPEC = (16 * HALF, 256)


def shape(*dims):
    return jax.ShapeDtypeStruct(dims, F32)


def body(raw_planes, offsets):
    rows3, back3, weight, cols3, twist = south_tables()
    rows3_e, back3_e, weight_e, cols3_e = east_tables()
    tables = (rows3, cols3, twist, rows3_e, back3_e, weight_e, cols3_e)
    fields, tile, strip, spec, east = pl.pallas_call(
        first_kernel,
        out_shape=(shape(2, ROWS, WIDTH), shape(PLANES, ROWS, WIDTH), shape(CUT, WIDTH), shape(*SPEC), shape(ROWS, CUT)),
        in_specs=[SMEM] + [HBM] * (1 + len(tables)),
        out_specs=(VMEM,) * 5,
        scratch_shapes=[
            pltpu.VMEM((ROWS, WIDTH), F32),
            pltpu.VMEM((ROWS, CUT), F32),
            pltpu.VMEM((CUT, WIDTH), F32),
            pltpu.VMEM((2, ROWS, WIDTH), F32),
            pltpu.VMEM((ROWS, WIDTH), F32),
            pltpu.VMEM((ROWS, WIDTH), F32),
            *[pltpu.VMEM((ROWS, w), F32) for w in WIDTHS],
            pltpu.VMEM((REACH, BLOCK, 128), F32),
            pltpu.VMEM((REACH, BLOCK, 128), F32),
            pltpu.VMEM((2, BLOCK, 128), F32),
            pltpu.VMEM((2 * HALF, WIDTH), F32),
            pltpu.VMEM(SPEC, F32),
            pltpu.VMEM((ROWS, 2 * CUT), F32),
            pltpu.SemaphoreType.DMA((CHAINS + len(tables),)),
            *[pltpu.VMEM(t.shape, t.dtype) for t in tables],
            pltpu.SemaphoreType.DMA((COPIES + 1,)),
            pltpu.SemaphoreType.DMA((COPIES + 1,)),
        ],
        compiler_params=pltpu.CompilerParams(collective_id=0, has_side_effects=True, vmem_limit_bytes=33 << 20),
        name="first",
    )(offsets, raw_planes[0], *tables)
    corrected, east_corr, south_corr = pl.pallas_call(
        south_kernel,
        out_shape=(shape(PLANES, ROWS, WIDTH), shape(ROWS, CUT), shape(CUT, WIDTH)),
        in_specs=[SMEM] + [VMEM] * 10,
        out_specs=(ANY, ANY, VMEM),
        scratch_shapes=[
            pltpu.VMEM((2 * HALF, WIDTH), F32),
            pltpu.VMEM(SPEC, F32),
            pltpu.VMEM(SPEC, F32),
            pltpu.VMEM((16 * HALF, 128), F32),
            pltpu.VMEM((PLANES, ROWS, WIDTH), F32),
            pltpu.VMEM((CUT, WIDTH), F32),
            pltpu.VMEM((CUT, WIDTH), F32),
            pltpu.SemaphoreType.DMA((2,)),
        ],
        compiler_params=pltpu.CompilerParams(vmem_limit_bytes=24 << 20),
        name="second",
    )(offsets, spec, tile, fields, strip, east, rows3, back3, weight, cols3, twist)
    return (corrected[None], east_corr[None], south_corr[None])


def solution(mesh):
    in_specs = (P(("gz", "ta"), None, None, None), P())
    out_specs = (
        P(("gz", "ta"), None, None, None),
        P(("gz", "ta"), None, None),
        P(("gz", "ta"), None, None),
    )
    return jax.shard_map(body, mesh=mesh, in_specs=in_specs, out_specs=out_specs, check_vma=False)
```

```python
import math

import jax
import jax.numpy as jnp
import ml_dtypes
import numpy as np
from jax import lax
from jax.experimental import pallas as pl
from jax.experimental.pallas import tpu as pltpu
from jax.sharding import PartitionSpec as P

ROWS = 320
WIDTH = 2048
CUT = 256
GRID_COLS = 8
TILES = 256
PLANES = 2
HALF = 144
EAST_HALF = 176
MESH = pl.DeviceIdType.MESH
F32 = jnp.float32
BF16 = jnp.bfloat16


def two_parts(table):
    high = table.astype(ml_dtypes.bfloat16)
    low = (table - high.astype(np.float64)).astype(ml_dtypes.bfloat16)
    return high, low


def three_parts(table):
    parts = []
    for _ in range(3):
        parts.append(table.astype(ml_dtypes.bfloat16))
        table = table - parts[-1].astype(table.dtype)
    return parts


def angles(rows, cols, length):
    product = np.outer(np.arange(rows), np.arange(cols)) % length
    return product * (2.0 * np.pi / length)


def row_tables(length, cols):
    count = length // 2 + 1
    turn = angles(count, length, length)
    weight = np.full((count, 1), 2.0)
    weight[0] = weight[-1] = 1.0
    scale = 1.0 / math.sqrt(length * cols)
    forward = np.cos(turn), -np.sin(turn)
    backward = (weight * np.cos(turn)).T * scale, (weight * np.sin(turn)).T * scale
    return forward, backward


AT_ROWS, AT_BACK, AT_EAST_ROWS, AT_EAST_BACK, AT_COLS, AT_TWIST, BUNDLE = 0, 256, 512, 864, 1184, 1696, 1728


def bundle():
    out = np.zeros((BUNDLE, 768), ml_dtypes.bfloat16)

    def put(row, col, table):
        out[row : row + table.shape[0], col : col + table.shape[1]] = table

    (cos, sin), (back_cos, back_sin) = row_tables(CUT, WIDTH)
    high, low = two_parts(np.concatenate([cos, sin[1:-1]]))
    put(AT_ROWS, 0, np.concatenate([high, high, low], axis=1))
    high, low = two_parts(np.concatenate([back_cos, back_sin[:, 1:-1]], axis=1))
    put(AT_BACK, 0, np.concatenate([high, high, low], axis=1))
    (cos, sin), (back_cos, back_sin) = row_tables(ROWS, CUT)
    whole = np.zeros((2 * EAST_HALF, ROWS))
    whole[: len(cos)], whole[EAST_HALF : EAST_HALF + len(sin)] = cos, sin
    for i, part in enumerate(two_parts(whole)):
        put(AT_EAST_ROWS, 384 * i, part)
    whole = np.zeros((ROWS, 2 * EAST_HALF))
    whole[:, : len(cos)], whole[:, EAST_HALF : EAST_HALF + len(sin)] = back_cos, back_sin
    for i, part in enumerate(two_parts(whole)):
        put(AT_EAST_BACK, 384 * i, part)
    turn = angles(CUT, CUT, CUT)
    for i, part in enumerate(two_parts(np.concatenate([np.cos(turn), np.sin(turn)], axis=1))):
        put(AT_COLS + CUT * i, 0, part)
    turn = angles(128, 128, 128)
    cos, sin = np.cos(turn), np.sin(turn)
    for i, part in enumerate(two_parts(np.block([[cos, -sin], [sin, cos]]))):
        put(AT_COLS + CUT * i, 512, part)
    turn = angles(16, 128, WIDTH)
    for i, part in enumerate(three_parts(np.concatenate([np.cos(turn), -np.sin(turn)]).astype(np.float32))):
        put(AT_TWIST, 128 * i, part)
    return out


def table_rows3(t):
    return t[AT_ROWS : AT_ROWS + 256, :]


def table_back3(t):
    return t[AT_BACK : AT_BACK + 256, :]


def table_cols3(t):
    high = t[AT_COLS : AT_COLS + 256, 512:]
    return jnp.concatenate([high, high, t[AT_COLS + 256 : AT_COLS + 512, 512:]], axis=0)


def table_twist(t):
    parts = [t[AT_TWIST : AT_TWIST + 32, 128 * i : 128 * i + 128].astype(F32) for i in range(3)]
    return (parts[0] + parts[1]) + parts[2]


def pair_of(t, row, rows, cols):
    return t[row : row + rows, :cols], t[row : row + rows, 384 : 384 + cols]


def dot(a, b):
    return jnp.dot(a, b, preferred_element_type=F32)


def three(x, axis):
    high, low = split(x)
    return jnp.concatenate([high, low, high], axis=axis)


def split(x):
    high = x.astype(BF16)
    return high, (x - high.astype(F32)).astype(BF16)


def left_dot(table, x):
    high, low = split(x)
    return dot(table[0], high) + (dot(table[0], low) + dot(table[1], high))


def right_dot(x, table):
    high, low = split(x)
    return dot(high, table[0]) + (dot(low, table[0]) + dot(high, table[1]))


def butterfly(re, im):
    size = len(re)
    if size == 1:
        return re, im
    even_re, even_im = butterfly(re[::2], im[::2])
    odd_re, odd_im = butterfly(re[1::2], im[1::2])
    top_re, top_im, low_re, low_im = [], [], [], []
    root = math.sqrt(0.5)
    for k in range(size // 2):
        a, b = odd_re[k], odd_im[k]
        if k == 0:
            pass
        elif 4 * k == size:
            a, b = b, -a
        elif 8 * k == size:
            a, b = root * (a + b), root * (b - a)
        elif 8 * k == 3 * size:
            a, b = root * (b - a), -root * (a + b)
        else:
            c, s = math.cos(2 * math.pi * k / size), math.sin(2 * math.pi * k / size)
            a, b = c * a + s * b, c * b - s * a
        top_re.append(even_re[k] + a)
        top_im.append(even_im[k] + b)
        low_re.append(even_re[k] - a)
        low_im.append(even_im[k] - b)
    return top_re + low_re, top_im + low_im


def at(start, size, step):
    return pl.ds(pl.multiple_of(start, step), size)


def loop(count, f):
    lax.fori_loop(0, count, lambda i, c: (f(i), c)[1], 0)


def moved(x, steps, axis):
    count = jnp.full(x.shape, steps, jnp.int32)
    for bit in (32, 16, 8, 4, 2, 1):
        x = jnp.where((count & bit) != 0, pltpu.roll(x, bit, axis), x)
    return x


def south_forward(strip_of, t, twist, y, z, spec):
    twist[...] = table_twist(t)
    for r in (128, HALF + 128):
        y[r : r + 16, :] = jnp.zeros((16, WIDTH), F32)
    top = lax.broadcasted_iota(jnp.int32, (8, 256), 0) == 0

    def rows_step(i):
        cols = at(i * 256, 256, 256)
        d = dot(table_rows3(t), three(strip_of(cols), 0))
        y[:128, cols] = d[:128]
        y[128:136, cols] = jnp.where(top, d[128:136], 0.0)
        y[HALF : HALF + 8, cols] = jnp.where(top, 0.0, d[128:136])
        y[HALF + 8 : HALF + 128, cols] = d[136:]

    loop(8, rows_step)

    def turn_step(i):
        top, low = at(i * 8, 8, 8), at(HALF + i * 8, 8, 8)
        re = [y[top, 128 * a : 128 * a + 128] for a in range(16)]
        im = [y[low, 128 * a : 128 * a + 128] for a in range(16)]
        re, im = butterfly(re, im)
        for k in range(16):
            c, s = twist[k : k + 1, :], twist[16 + k : 17 + k, :]
            to = at(k * HALF + i * 8, 8, 8)
            z[to, :128] = re[k] * c - im[k] * s
            z[to, 128:] = re[k] * s + im[k] * c

    loop(HALF // 8, turn_step)

    def cols_step(i):
        to = at(i * 576, 576, 8)
        spec[to, :] = dot(three(z[to, :], 1), table_cols3(t))

    loop(4, cols_step)


def half_weight(first, rows, last):
    h = first + lax.broadcasted_iota(jnp.int32, (rows, 128), 0)
    return jnp.where(h < last, jnp.where(h == 0, 1.0, 2.0), jnp.where(h == last, 1.0, 0.0))


def south_kernel(own, ready, east, strip, inv, dark, t, corrected, east_out, out, y, z, spec, mag, twist, sems):
    writes = [pltpu.make_async_copy(ready, corrected, sems.at[0]), pltpu.make_async_copy(east, east_out, sems.at[1])]
    for w in writes:
        w.start()

    def strip_of(cols):
        return (0.5 * strip[:, cols] - dark[:, cols]) * inv[:, cols]

    south_forward(strip_of, t, twist, y, z, spec)

    def cross_step(i, total):
        part = jnp.zeros((8, 128), F32)
        for k in range(16):
            here = at(k * HALF + i * 8, 8, 8)
            ar, ai = own[here, :128], own[here, 128:]
            br, bi = spec[here, :128], spec[here, 128:]
            cr = ar * br + ai * bi
            ci = ai * br - ar * bi
            size = jnp.sqrt(cr * cr + ci * ci)
            z[here, :128] = cr
            z[here, 128:] = -ci
            mag[here, :] = size
            part = part + size
        return total + part * half_weight(i * 8, 8, CUT // 2)

    total = lax.fori_loop(0, HALF // 8, cross_step, jnp.zeros((8, 128), F32))
    floor = jnp.sum(total) * (1.0 / (CUT * WIDTH)) + 1e-06

    def cols_step(i):
        here = at(i * 288, 288, 8)
        scale = 1.0 / (mag[here, :] + floor)
        x = jnp.concatenate([z[here, :128] * scale, z[here, 128:] * scale], axis=1)
        spec[here, :] = dot(three(x, 1), table_cols3(t))

    loop(8, cols_step)

    def turn_step(i):
        re, im = [], []
        for k in range(16):
            c, s = twist[k : k + 1, :], twist[16 + k : 17 + k, :]
            here = at(k * HALF + i * 8, 8, 8)
            a, b = spec[here, :128], spec[here, 128:]
            re.append(a * c - b * s)
            im.append(a * s + b * c)
        re, im = butterfly(re, im)
        top, low = at(i * 8, 8, 8), at(HALF + i * 8, 8, 8)
        for a in range(16):
            y[top, 128 * a : 128 * a + 128] = re[a]
            y[low, 128 * a : 128 * a + 128] = im[a]

    loop(HALF // 8, turn_step)

    top = lax.broadcasted_iota(jnp.int32, (8, 256), 0) == 0

    def rows_step(i):
        cols = at(i * 256, 256, 256)
        nyquist = y[128:136, cols]
        first = jnp.where(top, nyquist, y[HALF : HALF + 8, cols])
        x = jnp.concatenate([y[:128, cols], first, y[HALF + 8 : HALF + 128, cols]], axis=0)
        out[:, cols] = dot(table_back3(t), three(x, 0))

    loop(8, rows_step)
    for w in writes:
        w.wait()


def east_into(out, x, t):
    half = EAST_HALF
    y = left_dot(pair_of(t, AT_EAST_ROWS, 2 * half, ROWS), x)
    cols = t[AT_COLS : AT_COLS + CUT, :512], t[AT_COLS + CUT : AT_COLS + 2 * CUT, :512]

    def columns(v):
        p = right_dot(v, cols)
        return p[:half, :CUT] + p[half:, CUT:], p[half:, :CUT] - p[:half, CUT:]

    ar, ai = columns(y[:, :CUT])
    br, bi = columns(y[:, CUT:])
    cr = ar * br + ai * bi
    ci = ai * br - ar * bi
    size = jnp.sqrt(cr * cr + ci * ci)
    weighted = (size[:, :128] + size[:, 128:]) * half_weight(0, half, ROWS // 2)
    floor = jnp.sum(weighted) * (1.0 / (ROWS * CUT)) + 1e-06
    scale = 1.0 / (size + floor)
    vr, vi = columns(jnp.concatenate([cr * scale, -ci * scale], axis=0))
    out[...] = left_dot(pair_of(t, AT_EAST_BACK, ROWS, 2 * half), jnp.concatenate([vr, vi], axis=0))


CHAINS = 4
BAND = ROWS // CHAINS
RING = 8
BLOCK = ROWS // RING
WIDTHS = (1024, 512, 256, 128)
REACH = 3


def first_kernel(
    offsets, raw, bundled,
    tile, strip, spec, east, inv_south, dark_south, t,
    out, sums, west, mine, logs, acc, first, recv1, recv2, recv3, recv4, near, far, hop, spec_y, spec_z, both, twist,
    load, send, recv,
):
    gz, ta = lax.axis_index("gz"), lax.axis_index("ta")
    y, z = gz // 2, (ta // 8) * 2 + gz % 2
    x, core = (ta // 2) % 4, ta % 2
    other = 1 - core

    loads = []
    for q in range(CHAINS):
        band = pl.ds(q * BAND, BAND)
        c = pltpu.make_async_copy(raw.at[:, band], tile.at[:, band], load.at[q])
        c.start()
        loads.append(c)

    table_load = pltpu.make_async_copy(bundled, t, load.at[CHAINS])
    table_load.start()

    def device(x, y, z, core):
        z = (z + RING) % RING
        return (y * 2 + z % 2, (z // 2) * 8 + x * 2 + core)

    def beside(p):
        return p + 1 - 2 * (p % 2)

    def across(p):
        return 3 - p

    def gray(p):
        return (p + p // 2) % 2

    def upper(p):
        return p // 2

    def along(axis, move):
        on_x = (1 - core) if axis == 0 else core
        return device(x + on_x * (move(x) - x), y + (1 - on_x) * (move(y) - y), z, core)

    place = (x + core * (y - x), y + core * (x - y))
    partner_core = device(x, y, z, other)
    partner = {(axis, move): along(axis, move) for axis in (0, 1) for move in (beside, across)}
    down = [device(x, y, z - d, core) for d in range(1, REACH + 1)]
    up = [device(x, y, z + d, core) for d in range(1, REACH + 1)]
    count_ta = lax.axis_size("ta")
    before, after = (gz, (ta + count_ta - 1) % count_ta), (gz, (ta + 1) % count_ta)

    south = (gz, (ta + GRID_COLS) % count_ta)
    north = (gz, (ta + count_ta - GRID_COLS) % count_ta)
    has_south, has_north = ta < count_ta - GRID_COLS, ta >= GRID_COLS
    own_tile = gz * count_ta + ta

    barrier = pltpu.get_barrier_semaphore()
    everyone = [partner_core, *partner.values(), *down, *up, before, after, south, north]
    for d in everyone:
        pl.semaphore_signal(barrier, inc=1, device_id=d, device_id_type=MESH)

    count = [0]
    started = []

    def copy(src, dst, to):
        i = count[0]
        count[0] += 1
        c = pltpu.make_async_remote_copy(
            src_ref=src, dst_ref=dst, send_sem=send.at[i], recv_sem=recv.at[i], device_id=to, device_id_type=MESH
        )
        c.start()
        started.append(c)
        return c

    def band(q):
        return pl.ds(q * BAND, BAND)

    for q in range(CHAINS):
        loads[q].wait()

        def add_planes(i, q=q):
            r = at(q * BAND + i * 8, 8, 8)
            sums[r, :] = tile[0, r, :] + tile[1, r, :]

        loop(BAND // 8, add_planes)

    def cut(i):
        cols = at(i * 128, 128, 128)
        mine[:, cols] = moved(sums[:, cols], offsets[own_tile, 1], 0)[ROWS - CUT :]

    loop(WIDTH // 128, cut)
    pl.semaphore_wait(barrier, len(everyone))
    south_copy = pltpu.make_async_remote_copy(
        src_ref=mine, dst_ref=strip, send_sem=send.at[COPIES], recv_sem=recv.at[COPIES], device_id=south, device_id_type=MESH
    )

    @pl.when(has_south)
    def _():
        south_copy.start()

    @pl.when(jnp.logical_not(has_north))
    def _():
        strip[...] = jnp.zeros_like(strip)

    beside_copy = copy(sums.at[:, pl.ds(0, CUT)], west, before)

    orders = [
        [(0, beside, gray), (0, across, upper), (1, beside, gray), (1, across, upper)],
        [(0, across, upper), (0, beside, gray), (1, across, upper), (1, beside, gray)],
    ]
    moves = [orders[q % 2] for q in range(CHAINS)]
    into = [recv1, recv2, recv3, recv4]
    bases = [[0] for q in range(CHAINS)]
    flight = []
    for q in range(CHAINS):

        def take(i, q=q):
            r = at(q * BAND + i * 8, 8, 8)
            for c in range(0, WIDTH, 512):
                cols = slice(c, c + 512)
                one, two = jnp.log(tile[0, r, cols]), jnp.log(tile[1, r, cols])
                logs[0, r, cols] = one + two
                logs[1, r, cols] = jnp.minimum(one, two)

        loop(BAND // 8, take)
        bit = moves[q][0][2](place[1])
        halves = [at((1 - bit) * 1024, 1024, 128), at(bit * 1024, 1024, 128)]
        flight.append([copy(logs.at[other, band(q), c], first.at[band(q), c], partner_core) for c in halves])

    steps = len(WIDTHS)
    for q in range(CHAINS):

        def add_first(i, q=q, c=0):
            r = at(q * BAND + i * 8, 8, 8)
            acc[r, c] = logs[core, r, c] + first[r, c]

        halves = flight[q]
        axis, move, bit = moves[q][0]
        b = bit(place[axis])
        c = at((1 - b) * 1024, 1024, 128)
        halves[0].wait_recv()
        loop(BAND // 8, lambda i, q=q, c=c: add_first(i, q, c))
        flight[q] = copy(acc.at[band(q), c], into[0].at[band(q)], partner[(axis, move)])
        c = at(b * 1024, 1024, 128)
        halves[1].wait_recv()
        loop(BAND // 8, lambda i, q=q, c=c: add_first(i, q, c))
        bases[q].append(b * 1024)
    for step in range(1, steps + 1):
        for q in range(CHAINS):
            flight[q].wait_recv()
            w = WIDTHS[step - 1]

            def add_next(i, q=q, c=at(bases[q][step], w, 128), buf=into[step - 1]):
                r = at(q * BAND + i * 8, 8, 8)
                acc[r, c] = acc[r, c] + buf[r, :]

            loop(BAND // 8, add_next)
            if step < steps:
                axis, move, bit = moves[q][step]
                w = WIDTHS[step]
                b = bit(place[axis])
                base = bases[q][step]
                flight[q] = copy(
                    acc.at[band(q), at(base + (1 - b) * w, w, 128)], into[step].at[band(q)], partner[(axis, move)]
                )
                bases[q].append(base + b * w)

    def block(shift):
        j = (z + shift + RING) % RING
        col = bases[0][steps] + ((j // 2) % 2) * (bases[1][steps] - bases[0][steps])
        return at(j * BLOCK, BLOCK, 8), at(col, 128, 128)

    fars, nears = [], []
    for d in range(1, REACH + 1):
        r, c = block(4 - d)
        fars.append(copy(acc.at[r, c], far.at[d - 1], down[d - 1]))
    for d in range(1, REACH + 1):
        r, c = block(-d)
        nears.append(copy(acc.at[r, c], near.at[d - 1], down[d - 1]))
    for f in fars:
        f.wait_recv()
    r, c = block(4)
    acc[r, c] = (acc[r, c] + far[0]) + (far[1] + far[2])
    f = copy(acc.at[r, c], hop.at[0], down[2])
    f.wait_recv()
    f = copy(hop.at[0], hop.at[1], down[0])
    for n in nears:
        n.wait_recv()
    r, c = block(0)
    total = (acc[r, c] + near[0]) + (near[1] + near[2])
    f.wait_recv()
    total = total + hop[1]
    is_floor = core.astype(F32)
    scale = is_floor * (1.0 / TILES) - (1.0 - is_floor) * (1.0 / (TILES * PLANES))
    out[core, r, c] = (1.0 - 0.5 * is_floor) * jnp.exp(total * scale)

    def give(r, c, to):
        return copy(out.at[core, r, c], out.at[core, r, c], to)

    ones = [give(*block(0), to) for to in down]
    ones[0].wait_recv()
    f = give(*block(1), down[2])
    f.wait_recv()
    fours = [give(*block(4), to) for to in down]
    for f in ones[1:] + fours:
        f.wait_recv()
    passed = []

    def pass_on(q, base, w):
        passed.append(give(band(q), at(base, w, 128), partner_core))

    for step in range(steps - 1, -1, -1):
        for q in range(CHAINS):
            w = WIDTHS[step]
            if step < steps - 1:
                flight[q].wait_recv()
            axis, move, _ = moves[q][step]
            flight[q] = give(band(q), at(bases[q][step + 1], w, 128), partner[(axis, move)])
            if step == steps - 1:
                pass_on(q, bases[q][steps], w)
            else:
                pass_on(q, 2 * bases[q][step + 1] + WIDTHS[step + 1] - bases[q][step + 2], WIDTHS[step + 1])
    for q in range(CHAINS):
        flight[q].wait_recv()
        pass_on(q, WIDTHS[0] - bases[q][1], WIDTHS[0])
    for c in passed:
        c.wait_recv()
    beside_copy.wait_recv()

    table_load.wait()

    def own_of(cols):
        return (0.5 * sums[:CUT, cols] - out[1, :CUT, cols]) * out[0, :CUT, cols]

    south_forward(own_of, t, twist, spec_y, spec_z, spec)
    has_east = (ta < count_ta - 1).astype(F32)

    def strips(i):
        r, last = at(i * 64, 64, 64), slice(WIDTH - 3 * 128, WIDTH)
        eastern = (0.5 * sums[r, last] - out[1, r, last]) * out[0, r, last]
        both[r, :CUT] = moved(eastern, offsets[own_tile, 0], 1)[:, 128:]
        both[r, CUT:] = (0.5 * west[r, :] - out[1, r, :CUT]) * out[0, r, :CUT] * has_east

    loop(ROWS // 64, strips)
    east_into(east, both[...], t)

    def correct(i):
        r = at(i * 8, 8, 8)
        for c in range(0, WIDTH, 512):
            cols = slice(c, c + 512)
            g, d = out[0, r, cols], out[1, r, cols]
            for p in range(PLANES):
                tile[p, r, cols] = (tile[p, r, cols] - d) * g

    loop(ROWS // 8, correct)
    north_tile = jnp.maximum(own_tile - GRID_COLS, 0)
    north_is = has_north.astype(F32)

    def cut_fields(i):
        cols = at(i * 128, 128, 128)
        steps = offsets[north_tile, 1]
        inv_south[:, cols] = moved(out[0, :, cols], steps, 0)[ROWS - CUT :] * north_is
        dark_south[:, cols] = moved(out[1, :, cols], steps, 0)[ROWS - CUT :]

    loop(WIDTH // 128, cut_fields)

    @pl.when(has_north)
    def _():
        south_copy.wait_recv()

    for c in started:
        c.wait_send()

    @pl.when(has_south)
    def _():
        south_copy.wait_send()


COPIES = CHAINS * (2 * len(WIDTHS) + 2 + len(WIDTHS) + 1) + 1 + (2 * REACH + 2) + (2 * REACH + 1)


VMEM = pl.BlockSpec(memory_space=pltpu.VMEM)
SMEM = pl.BlockSpec(memory_space=pltpu.SMEM)
ANY = pl.BlockSpec(memory_space=pl.ANY)
HBM = pl.BlockSpec(memory_space=pltpu.HBM)
SPEC = (16 * HALF, 256)
FIRST_LIMIT = 34


def shape(*dims):
    return jax.ShapeDtypeStruct(dims, F32)


def body(raw_planes, offsets):
    table = jax.ShapeDtypeStruct((BUNDLE, 768), BF16)
    ready, strip, spec, east, inv, dark, tables = pl.pallas_call(
        first_kernel,
        out_shape=(
            shape(PLANES, ROWS, WIDTH), shape(CUT, WIDTH), shape(*SPEC), shape(ROWS, CUT), shape(CUT, WIDTH), shape(CUT, WIDTH), table,
        ),
        in_specs=[SMEM, ANY, ANY],
        out_specs=(VMEM,) * 7,
        scratch_shapes=[
            pltpu.VMEM((2, ROWS, WIDTH), F32),
            pltpu.VMEM((ROWS, WIDTH), F32),
            pltpu.VMEM((ROWS, CUT), F32),
            pltpu.VMEM((CUT, WIDTH), F32),
            pltpu.VMEM((2, ROWS, WIDTH), F32),
            pltpu.VMEM((ROWS, WIDTH), F32),
            pltpu.VMEM((ROWS, WIDTH), F32),
            *[pltpu.VMEM((ROWS, w), F32) for w in WIDTHS],
            pltpu.VMEM((REACH, BLOCK, 128), F32),
            pltpu.VMEM((REACH, BLOCK, 128), F32),
            pltpu.VMEM((2, BLOCK, 128), F32),
            pltpu.VMEM((2 * HALF, WIDTH), F32),
            pltpu.VMEM(SPEC, F32),
            pltpu.VMEM((ROWS, 2 * CUT), F32),
            pltpu.VMEM((32, 128), F32),
            pltpu.SemaphoreType.DMA((CHAINS + 1,)),
            pltpu.SemaphoreType.DMA((COPIES + 1,)),
            pltpu.SemaphoreType.DMA((COPIES + 1,)),
        ],
        compiler_params=pltpu.CompilerParams(collective_id=0, has_side_effects=True, vmem_limit_bytes=FIRST_LIMIT << 20),
        name="first",
    )(offsets, raw_planes[0], bundle())
    corrected, east_corr, south_corr = pl.pallas_call(
        south_kernel,
        out_shape=(shape(PLANES, ROWS, WIDTH), shape(ROWS, CUT), shape(CUT, WIDTH)),
        in_specs=[VMEM] * 7,
        out_specs=(ANY, ANY, VMEM),
        scratch_shapes=[
            pltpu.VMEM((2 * HALF, WIDTH), F32),
            pltpu.VMEM(SPEC, F32),
            pltpu.VMEM(SPEC, F32),
            pltpu.VMEM((16 * HALF, 128), F32),
            pltpu.VMEM((32, 128), F32),
            pltpu.SemaphoreType.DMA((2,)),
        ],
        compiler_params=pltpu.CompilerParams(vmem_limit_bytes=20 << 20),
        name="second",
    )(spec, ready, east, strip, inv, dark, tables)
    return (corrected[None], east_corr[None], south_corr[None])


def solution(mesh):
    in_specs = (P(("gz", "ta"), None, None, None), P())
    out_specs = (
        P(("gz", "ta"), None, None, None),
        P(("gz", "ta"), None, None),
        P(("gz", "ta"), None, None),
    )
    return jax.shard_map(body, mesh=mesh, in_specs=in_specs, out_specs=out_specs, check_vma=False)
```

```python
import math

import jax
import jax.numpy as jnp
import ml_dtypes
import numpy as np
from jax import lax
from jax.experimental import pallas as pl
from jax.experimental.pallas import tpu as pltpu
from jax.sharding import PartitionSpec as P

ROWS = 320
WIDTH = 2048
CUT = 256
GRID_COLS = 8
TILES = 256
PLANES = 2
HALF = 144
EAST_HALF = 176
MESH = pl.DeviceIdType.MESH
F32 = jnp.float32
U_ROWS, U_COLS, U_TURN = 8, 4, 1
BF16 = jnp.bfloat16


def two_parts(table):
    high = table.astype(ml_dtypes.bfloat16)
    low = (table - high.astype(np.float64)).astype(ml_dtypes.bfloat16)
    return high, low


def three_parts(table):
    parts = []
    for _ in range(3):
        parts.append(table.astype(ml_dtypes.bfloat16))
        table = table - parts[-1].astype(table.dtype)
    return parts


def angles(rows, cols, length):
    product = np.outer(np.arange(rows), np.arange(cols)) % length
    return product * (2.0 * np.pi / length)


def row_tables(length, cols):
    count = length // 2 + 1
    turn = angles(count, length, length)
    weight = np.full((count, 1), 2.0)
    weight[0] = weight[-1] = 1.0
    scale = 1.0 / math.sqrt(length * cols)
    forward = np.cos(turn), -np.sin(turn)
    backward = (weight * np.cos(turn)).T * scale, (weight * np.sin(turn)).T * scale
    return forward, backward


AT_ROWS, AT_BACK, AT_EAST_ROWS, AT_EAST_BACK, AT_COLS, AT_TWIST, BUNDLE = 0, 256, 512, 864, 1184, 1696, 1728


def bundle():
    out = np.zeros((BUNDLE, 768), ml_dtypes.bfloat16)

    def put(row, col, table):
        out[row : row + table.shape[0], col : col + table.shape[1]] = table

    (cos, sin), (back_cos, back_sin) = row_tables(CUT, WIDTH)
    high, low = two_parts(np.concatenate([cos, sin[1:-1]]))
    put(AT_ROWS, 0, np.concatenate([high, high, low], axis=1))
    high, low = two_parts(np.concatenate([back_cos, back_sin[:, 1:-1]], axis=1))
    put(AT_BACK, 0, np.concatenate([high, high, low], axis=1))
    (cos, sin), (back_cos, back_sin) = row_tables(ROWS, CUT)
    whole = np.zeros((2 * EAST_HALF, ROWS))
    whole[: len(cos)], whole[EAST_HALF : EAST_HALF + len(sin)] = cos, sin
    for i, part in enumerate(two_parts(whole)):
        put(AT_EAST_ROWS, 384 * i, part)
    whole = np.zeros((ROWS, 2 * EAST_HALF))
    whole[:, : len(cos)], whole[:, EAST_HALF : EAST_HALF + len(sin)] = back_cos, back_sin
    for i, part in enumerate(two_parts(whole)):
        put(AT_EAST_BACK, 384 * i, part)
    turn = angles(CUT, CUT, CUT)
    for i, part in enumerate(two_parts(np.concatenate([np.cos(turn), np.sin(turn)], axis=1))):
        put(AT_COLS + CUT * i, 0, part)
    turn = angles(128, 128, 128)
    cos, sin = np.cos(turn), np.sin(turn)
    for i, part in enumerate(two_parts(np.block([[cos, -sin], [sin, cos]]))):
        put(AT_COLS + CUT * i, 512, part)
    turn = angles(16, 128, WIDTH)
    for i, part in enumerate(three_parts(np.concatenate([np.cos(turn), -np.sin(turn)]).astype(np.float32))):
        put(AT_TWIST, 128 * i, part)
    return out


def table_rows3(t):
    return t[AT_ROWS : AT_ROWS + 256, :]


def table_back3(t):
    return t[AT_BACK : AT_BACK + 256, :]


def table_cols3(t):
    high = t[AT_COLS : AT_COLS + 256, 512:]
    return jnp.concatenate([high, high, t[AT_COLS + 256 : AT_COLS + 512, 512:]], axis=0)


def table_twist(t):
    parts = [t[AT_TWIST : AT_TWIST + 32, 128 * i : 128 * i + 128].astype(F32) for i in range(3)]
    return (parts[0] + parts[1]) + parts[2]


def pair_of(t, row, rows, cols):
    return t[row : row + rows, :cols], t[row : row + rows, 384 : 384 + cols]


def dot(a, b):
    return jnp.dot(a, b, preferred_element_type=F32)


def three(x, axis):
    high, low = split(x)
    return jnp.concatenate([high, low, high], axis=axis)


def split(x):
    high = x.astype(BF16)
    return high, (x - high.astype(F32)).astype(BF16)


def left_dot(table, x):
    high, low = split(x)
    return dot(table[0], high) + (dot(table[0], low) + dot(table[1], high))


def right_dot(x, table):
    high, low = split(x)
    return dot(high, table[0]) + (dot(low, table[0]) + dot(high, table[1]))


def butterfly(re, im):
    size = len(re)
    if size == 1:
        return re, im
    even_re, even_im = butterfly(re[::2], im[::2])
    odd_re, odd_im = butterfly(re[1::2], im[1::2])
    top_re, top_im, low_re, low_im = [], [], [], []
    root = math.sqrt(0.5)
    for k in range(size // 2):
        a, b = odd_re[k], odd_im[k]
        if k == 0:
            pass
        elif 4 * k == size:
            a, b = b, -a
        elif 8 * k == size:
            a, b = root * (a + b), root * (b - a)
        elif 8 * k == 3 * size:
            a, b = root * (b - a), -root * (a + b)
        else:
            c, s = math.cos(2 * math.pi * k / size), math.sin(2 * math.pi * k / size)
            a, b = c * a + s * b, c * b - s * a
        top_re.append(even_re[k] + a)
        top_im.append(even_im[k] + b)
        low_re.append(even_re[k] - a)
        low_im.append(even_im[k] - b)
    return top_re + low_re, top_im + low_im


def at(start, size, step):
    return pl.ds(pl.multiple_of(start, step), size)


def loop(count, f, at_once=1):
    def step(i, c):
        for j in range(at_once):
            f(i * at_once + j)
        return c

    lax.fori_loop(0, count // at_once, step, 0)


def moved(x, steps, axis):
    count = jnp.full(x.shape, steps, jnp.int32)
    for bit in (32, 16, 8, 4, 2, 1):
        x = jnp.where((count & bit) != 0, pltpu.roll(x, bit, axis), x)
    return x


def south_forward(strip_of, t, twist, y, z, spec):
    twist[...] = table_twist(t)
    for r in (128, HALF + 128):
        y[r : r + 16, :] = jnp.zeros((16, WIDTH), F32)
    top = lax.broadcasted_iota(jnp.int32, (8, 256), 0) == 0

    def rows_step(i):
        cols = at(i * 256, 256, 256)
        d = dot(table_rows3(t), three(strip_of(cols), 0))
        y[:128, cols] = d[:128]
        y[128:136, cols] = jnp.where(top, d[128:136], 0.0)
        y[HALF : HALF + 8, cols] = jnp.where(top, 0.0, d[128:136])
        y[HALF + 8 : HALF + 128, cols] = d[136:]

    loop(8, rows_step, U_ROWS)

    def turn_step(i):
        top, low = at(i * 8, 8, 8), at(HALF + i * 8, 8, 8)
        re = [y[top, 128 * a : 128 * a + 128] for a in range(16)]
        im = [y[low, 128 * a : 128 * a + 128] for a in range(16)]
        re, im = butterfly(re, im)
        for k in range(16):
            c, s = twist[k : k + 1, :], twist[16 + k : 17 + k, :]
            to = at(k * HALF + i * 8, 8, 8)
            z[to, :128] = re[k] * c - im[k] * s
            z[to, 128:] = re[k] * s + im[k] * c

    loop(HALF // 8, turn_step, U_TURN)

    def cols_step(i):
        to = at(i * 576, 576, 8)
        spec[to, :] = dot(three(z[to, :], 1), table_cols3(t))

    loop(4, cols_step, U_COLS)


def half_weight(first, rows, last):
    h = first + lax.broadcasted_iota(jnp.int32, (rows, 128), 0)
    return jnp.where(h < last, jnp.where(h == 0, 1.0, 2.0), jnp.where(h == last, 1.0, 0.0))


def south_kernel(own, ready, east, strip, inv, dark, t, corrected, east_out, out, y, z, spec, mag, twist, sems):
    writes = [pltpu.make_async_copy(ready, corrected, sems.at[0]), pltpu.make_async_copy(east, east_out, sems.at[1])]
    for w in writes:
        w.start()

    def strip_of(cols):
        return (0.5 * strip[:, cols] - dark[:, cols]) * inv[:, cols]

    south_forward(strip_of, t, twist, y, z, spec)

    def cross_step(i, total):
        part = jnp.zeros((8, 128), F32)
        for k in range(16):
            here = at(k * HALF + i * 8, 8, 8)
            ar, ai = own[here, :128], own[here, 128:]
            br, bi = spec[here, :128], spec[here, 128:]
            cr = ar * br + ai * bi
            ci = ai * br - ar * bi
            size = jnp.sqrt(cr * cr + ci * ci)
            z[here, :128] = cr
            z[here, 128:] = -ci
            mag[here, :] = size
            part = part + size
        return total + part * half_weight(i * 8, 8, CUT // 2)

    total = lax.fori_loop(0, HALF // 8, cross_step, jnp.zeros((8, 128), F32))
    floor = jnp.sum(total) * (1.0 / (CUT * WIDTH)) + 1e-06

    def cols_step(i):
        here = at(i * 288, 288, 8)
        scale = 1.0 / (mag[here, :] + floor)
        x = jnp.concatenate([z[here, :128] * scale, z[here, 128:] * scale], axis=1)
        spec[here, :] = dot(three(x, 1), table_cols3(t))

    loop(8, cols_step, 2 * U_COLS)

    def turn_step(i):
        re, im = [], []
        for k in range(16):
            c, s = twist[k : k + 1, :], twist[16 + k : 17 + k, :]
            here = at(k * HALF + i * 8, 8, 8)
            a, b = spec[here, :128], spec[here, 128:]
            re.append(a * c - b * s)
            im.append(a * s + b * c)
        re, im = butterfly(re, im)
        top, low = at(i * 8, 8, 8), at(HALF + i * 8, 8, 8)
        for a in range(16):
            y[top, 128 * a : 128 * a + 128] = re[a]
            y[low, 128 * a : 128 * a + 128] = im[a]

    loop(HALF // 8, turn_step, U_TURN)

    top = lax.broadcasted_iota(jnp.int32, (8, 256), 0) == 0

    def rows_step(i):
        cols = at(i * 256, 256, 256)
        nyquist = y[128:136, cols]
        first = jnp.where(top, nyquist, y[HALF : HALF + 8, cols])
        x = jnp.concatenate([y[:128, cols], first, y[HALF + 8 : HALF + 128, cols]], axis=0)
        out[:, cols] = dot(table_back3(t), three(x, 0))

    loop(8, rows_step, U_ROWS)
    for w in writes:
        w.wait()


def east_into(out, x, t):
    half = EAST_HALF
    y = left_dot(pair_of(t, AT_EAST_ROWS, 2 * half, ROWS), x)
    cols = t[AT_COLS : AT_COLS + CUT, :512], t[AT_COLS + CUT : AT_COLS + 2 * CUT, :512]

    def columns(v):
        p = right_dot(v, cols)
        return p[:half, :CUT] + p[half:, CUT:], p[half:, :CUT] - p[:half, CUT:]

    ar, ai = columns(y[:, :CUT])
    br, bi = columns(y[:, CUT:])
    cr = ar * br + ai * bi
    ci = ai * br - ar * bi
    size = jnp.sqrt(cr * cr + ci * ci)
    weighted = (size[:, :128] + size[:, 128:]) * half_weight(0, half, ROWS // 2)
    floor = jnp.sum(weighted) * (1.0 / (ROWS * CUT)) + 1e-06
    scale = 1.0 / (size + floor)
    vr, vi = columns(jnp.concatenate([cr * scale, -ci * scale], axis=0))
    out[...] = left_dot(pair_of(t, AT_EAST_BACK, ROWS, 2 * half), jnp.concatenate([vr, vi], axis=0))


CHAINS = 4
BAND = ROWS // CHAINS
RING = 8
BLOCK = ROWS // RING
WIDTHS = (1024, 512, 256, 128)
REACH = 3


def first_kernel(
    offsets, raw, bundled,
    tile, strip, spec, east, inv_south, dark_south, t,
    out, sums, west, mine, logs, acc, first, recv1, recv2, recv3, recv4, near, far, hop, spec_y, spec_z, both, twist,
    load, send, recv,
):
    gz, ta = lax.axis_index("gz"), lax.axis_index("ta")
    y, z = gz // 2, (ta // 8) * 2 + gz % 2
    x, core = (ta // 2) % 4, ta % 2
    other = 1 - core

    loads = []
    for q in range(CHAINS):
        band = pl.ds(q * BAND, BAND)
        c = pltpu.make_async_copy(raw.at[:, band], tile.at[:, band], load.at[q])
        c.start()
        loads.append(c)

    table_load = pltpu.make_async_copy(bundled, t, load.at[CHAINS])
    table_load.start()

    def device(x, y, z, core):
        z = (z + RING) % RING
        return (y * 2 + z % 2, (z // 2) * 8 + x * 2 + core)

    def beside(p):
        return p + 1 - 2 * (p % 2)

    def across(p):
        return 3 - p

    def gray(p):
        return (p + p // 2) % 2

    def upper(p):
        return p // 2

    def along(axis, move):
        on_x = (1 - core) if axis == 0 else core
        return device(x + on_x * (move(x) - x), y + (1 - on_x) * (move(y) - y), z, core)

    place = (x + core * (y - x), y + core * (x - y))
    partner_core = device(x, y, z, other)
    partner = {(axis, move): along(axis, move) for axis in (0, 1) for move in (beside, across)}
    down = [device(x, y, z - d, core) for d in range(1, REACH + 1)]
    up = [device(x, y, z + d, core) for d in range(1, REACH + 1)]
    count_ta = lax.axis_size("ta")
    before, after = (gz, (ta + count_ta - 1) % count_ta), (gz, (ta + 1) % count_ta)

    south = (gz, (ta + GRID_COLS) % count_ta)
    north = (gz, (ta + count_ta - GRID_COLS) % count_ta)
    has_south, has_north = ta < count_ta - GRID_COLS, ta >= GRID_COLS
    own_tile = gz * count_ta + ta

    barrier = pltpu.get_barrier_semaphore()
    everyone = [partner_core, *partner.values(), *down, *up, before, after, south, north]
    for d in everyone:
        pl.semaphore_signal(barrier, inc=1, device_id=d, device_id_type=MESH)

    count = [0]
    started = []

    def copy(src, dst, to):
        i = count[0]
        count[0] += 1
        c = pltpu.make_async_remote_copy(
            src_ref=src, dst_ref=dst, send_sem=send.at[i], recv_sem=recv.at[i], device_id=to, device_id_type=MESH
        )
        c.start()
        started.append(c)
        return c

    def band(q):
        return pl.ds(q * BAND, BAND)

    for q in range(CHAINS):
        loads[q].wait()

        def add_planes(i, q=q):
            r = at(q * BAND + i * 8, 8, 8)
            sums[r, :] = tile[0, r, :] + tile[1, r, :]

        loop(BAND // 8, add_planes)

    def cut(i):
        cols = at(i * 128, 128, 128)
        mine[:, cols] = moved(sums[:, cols], offsets[own_tile, 1], 0)[ROWS - CUT :]

    loop(WIDTH // 128, cut)
    pl.semaphore_wait(barrier, len(everyone))
    south_copy = pltpu.make_async_remote_copy(
        src_ref=mine, dst_ref=strip, send_sem=send.at[COPIES], recv_sem=recv.at[COPIES], device_id=south, device_id_type=MESH
    )

    @pl.when(has_south)
    def _():
        south_copy.start()

    @pl.when(jnp.logical_not(has_north))
    def _():
        strip[...] = jnp.zeros_like(strip)

    beside_copy = copy(sums.at[:, pl.ds(0, CUT)], west, before)

    orders = [
        [(0, beside, gray), (0, across, upper), (1, beside, gray), (1, across, upper)],
        [(0, across, upper), (0, beside, gray), (1, across, upper), (1, beside, gray)],
    ]
    moves = [orders[q % 2] for q in range(CHAINS)]
    into = [recv1, recv2, recv3, recv4]
    bases = [[0] for q in range(CHAINS)]
    flight = []
    for q in range(CHAINS):

        def take(i, q=q):
            r = at(q * BAND + i * 8, 8, 8)
            for c in range(0, WIDTH, 512):
                cols = slice(c, c + 512)
                one, two = jnp.log(tile[0, r, cols]), jnp.log(tile[1, r, cols])
                logs[0, r, cols] = one + two
                logs[1, r, cols] = jnp.minimum(one, two)

        loop(BAND // 8, take)
        bit = moves[q][0][2](place[1])
        halves = [at((1 - bit) * 1024, 1024, 128), at(bit * 1024, 1024, 128)]
        flight.append([copy(logs.at[other, band(q), c], first.at[band(q), c], partner_core) for c in halves])

    steps = len(WIDTHS)
    for q in range(CHAINS):

        def add_first(i, q=q, c=0):
            r = at(q * BAND + i * 8, 8, 8)
            acc[r, c] = logs[core, r, c] + first[r, c]

        halves = flight[q]
        axis, move, bit = moves[q][0]
        b = bit(place[axis])
        c = at((1 - b) * 1024, 1024, 128)
        halves[0].wait_recv()
        loop(BAND // 8, lambda i, q=q, c=c: add_first(i, q, c))
        flight[q] = copy(acc.at[band(q), c], into[0].at[band(q)], partner[(axis, move)])
        c = at(b * 1024, 1024, 128)
        halves[1].wait_recv()
        loop(BAND // 8, lambda i, q=q, c=c: add_first(i, q, c))
        bases[q].append(b * 1024)
    for step in range(1, steps + 1):
        for q in range(CHAINS):
            flight[q].wait_recv()
            w = WIDTHS[step - 1]

            def add_next(i, q=q, c=at(bases[q][step], w, 128), buf=into[step - 1]):
                r = at(q * BAND + i * 8, 8, 8)
                acc[r, c] = acc[r, c] + buf[r, :]

            loop(BAND // 8, add_next)
            if step < steps:
                axis, move, bit = moves[q][step]
                w = WIDTHS[step]
                b = bit(place[axis])
                base = bases[q][step]
                flight[q] = copy(
                    acc.at[band(q), at(base + (1 - b) * w, w, 128)], into[step].at[band(q)], partner[(axis, move)]
                )
                bases[q].append(base + b * w)

    def block(shift):
        j = (z + shift + RING) % RING
        col = bases[0][steps] + ((j // 2) % 2) * (bases[1][steps] - bases[0][steps])
        return at(j * BLOCK, BLOCK, 8), at(col, 128, 128)

    fars, nears = [], []
    for d in range(1, REACH + 1):
        r, c = block(4 - d)
        fars.append(copy(acc.at[r, c], far.at[d - 1], down[d - 1]))
    for d in range(1, REACH + 1):
        r, c = block(-d)
        nears.append(copy(acc.at[r, c], near.at[d - 1], down[d - 1]))
    for f in fars:
        f.wait_recv()
    r, c = block(4)
    acc[r, c] = (acc[r, c] + far[0]) + (far[1] + far[2])
    f = copy(acc.at[r, c], hop.at[0], down[2])
    f.wait_recv()
    f = copy(hop.at[0], hop.at[1], down[0])
    for n in nears:
        n.wait_recv()
    r, c = block(0)
    total = (acc[r, c] + near[0]) + (near[1] + near[2])
    f.wait_recv()
    total = total + hop[1]
    is_floor = core.astype(F32)
    scale = is_floor * (1.0 / TILES) - (1.0 - is_floor) * (1.0 / (TILES * PLANES))
    out[core, r, c] = (1.0 - 0.5 * is_floor) * jnp.exp(total * scale)

    def give(r, c, to):
        return copy(out.at[core, r, c], out.at[core, r, c], to)

    ones = [give(*block(0), to) for to in down]
    ones[0].wait_recv()
    f = give(*block(1), down[2])
    f.wait_recv()
    fours = [give(*block(4), to) for to in down]
    for f in ones[1:] + fours:
        f.wait_recv()
    passed = []

    def pass_on(q, base, w):
        passed.append(give(band(q), at(base, w, 128), partner_core))

    for step in range(steps - 1, -1, -1):
        for q in range(CHAINS):
            w = WIDTHS[step]
            if step < steps - 1:
                flight[q].wait_recv()
            axis, move, _ = moves[q][step]
            flight[q] = give(band(q), at(bases[q][step + 1], w, 128), partner[(axis, move)])
            if step == steps - 1:
                pass_on(q, bases[q][steps], w)
            else:
                pass_on(q, 2 * bases[q][step + 1] + WIDTHS[step + 1] - bases[q][step + 2], WIDTHS[step + 1])
    for q in range(CHAINS):
        flight[q].wait_recv()
        pass_on(q, WIDTHS[0] - bases[q][1], WIDTHS[0])
    for c in passed:
        c.wait_recv()
    beside_copy.wait_recv()

    table_load.wait()

    def own_of(cols):
        return (0.5 * sums[:CUT, cols] - out[1, :CUT, cols]) * out[0, :CUT, cols]

    south_forward(own_of, t, twist, spec_y, spec_z, spec)
    has_east = (ta < count_ta - 1).astype(F32)

    def strips(i):
        r, last = at(i * 64, 64, 64), slice(WIDTH - 3 * 128, WIDTH)
        eastern = (0.5 * sums[r, last] - out[1, r, last]) * out[0, r, last]
        both[r, :CUT] = moved(eastern, offsets[own_tile, 0], 1)[:, 128:]
        both[r, CUT:] = (0.5 * west[r, :] - out[1, r, :CUT]) * out[0, r, :CUT] * has_east

    loop(ROWS // 64, strips)
    east_into(east, both[...], t)

    def correct(i):
        r = at(i * 8, 8, 8)
        for c in range(0, WIDTH, 512):
            cols = slice(c, c + 512)
            g, d = out[0, r, cols], out[1, r, cols]
            for p in range(PLANES):
                tile[p, r, cols] = (tile[p, r, cols] - d) * g

    loop(ROWS // 8, correct)
    north_tile = jnp.maximum(own_tile - GRID_COLS, 0)
    north_is = has_north.astype(F32)

    def cut_fields(i):
        cols = at(i * 128, 128, 128)
        steps = offsets[north_tile, 1]
        inv_south[:, cols] = moved(out[0, :, cols], steps, 0)[ROWS - CUT :] * north_is
        dark_south[:, cols] = moved(out[1, :, cols], steps, 0)[ROWS - CUT :]

    loop(WIDTH // 128, cut_fields)

    @pl.when(has_north)
    def _():
        south_copy.wait_recv()

    for c in started:
        c.wait_send()

    @pl.when(has_south)
    def _():
        south_copy.wait_send()


COPIES = CHAINS * (2 * len(WIDTHS) + 2 + len(WIDTHS) + 1) + 1 + (2 * REACH + 2) + (2 * REACH + 1)


VMEM = pl.BlockSpec(memory_space=pltpu.VMEM)
SMEM = pl.BlockSpec(memory_space=pltpu.SMEM)
ANY = pl.BlockSpec(memory_space=pl.ANY)
HBM = pl.BlockSpec(memory_space=pltpu.HBM)
SPEC = (16 * HALF, 256)
FIRST_LIMIT = 34


def shape(*dims):
    return jax.ShapeDtypeStruct(dims, F32)


def body(raw_planes, offsets):
    table = jax.ShapeDtypeStruct((BUNDLE, 768), BF16)
    ready, strip, spec, east, inv, dark, tables = pl.pallas_call(
        first_kernel,
        out_shape=(
            shape(PLANES, ROWS, WIDTH), shape(CUT, WIDTH), shape(*SPEC), shape(ROWS, CUT), shape(CUT, WIDTH), shape(CUT, WIDTH), table,
        ),
        in_specs=[SMEM, ANY, ANY],
        out_specs=(VMEM,) * 7,
        scratch_shapes=[
            pltpu.VMEM((2, ROWS, WIDTH), F32),
            pltpu.VMEM((ROWS, WIDTH), F32),
            pltpu.VMEM((ROWS, CUT), F32),
            pltpu.VMEM((CUT, WIDTH), F32),
            pltpu.VMEM((2, ROWS, WIDTH), F32),
            pltpu.VMEM((ROWS, WIDTH), F32),
            pltpu.VMEM((ROWS, WIDTH), F32),
            *[pltpu.VMEM((ROWS, w), F32) for w in WIDTHS],
            pltpu.VMEM((REACH, BLOCK, 128), F32),
            pltpu.VMEM((REACH, BLOCK, 128), F32),
            pltpu.VMEM((2, BLOCK, 128), F32),
            pltpu.VMEM((2 * HALF, WIDTH), F32),
            pltpu.VMEM(SPEC, F32),
            pltpu.VMEM((ROWS, 2 * CUT), F32),
            pltpu.VMEM((32, 128), F32),
            pltpu.SemaphoreType.DMA((CHAINS + 1,)),
            pltpu.SemaphoreType.DMA((COPIES + 1,)),
            pltpu.SemaphoreType.DMA((COPIES + 1,)),
        ],
        compiler_params=pltpu.CompilerParams(collective_id=0, has_side_effects=True, vmem_limit_bytes=FIRST_LIMIT << 20),
        name="first",
    )(offsets, raw_planes[0], bundle())
    corrected, east_corr, south_corr = pl.pallas_call(
        south_kernel,
        out_shape=(shape(PLANES, ROWS, WIDTH), shape(ROWS, CUT), shape(CUT, WIDTH)),
        in_specs=[VMEM] * 7,
        out_specs=(ANY, ANY, VMEM),
        scratch_shapes=[
            pltpu.VMEM((2 * HALF, WIDTH), F32),
            pltpu.VMEM(SPEC, F32),
            pltpu.VMEM(SPEC, F32),
            pltpu.VMEM((16 * HALF, 128), F32),
            pltpu.VMEM((32, 128), F32),
            pltpu.SemaphoreType.DMA((2,)),
        ],
        compiler_params=pltpu.CompilerParams(vmem_limit_bytes=20 << 20),
        name="second",
    )(spec, ready, east, strip, inv, dark, tables)
    return (corrected[None], east_corr[None], south_corr[None])


def solution(mesh):
    in_specs = (P(("gz", "ta"), None, None, None), P())
    out_specs = (
        P(("gz", "ta"), None, None, None),
        P(("gz", "ta"), None, None),
        P(("gz", "ta"), None, None),
    )
    return jax.shard_map(body, mesh=mesh, in_specs=in_specs, out_specs=out_specs, check_vma=False)
```

```python
import math

import jax
import jax.numpy as jnp
import ml_dtypes
import numpy as np
from jax import lax
from jax.experimental import pallas as pl
from jax.experimental.pallas import tpu as pltpu
from jax.sharding import PartitionSpec as P

ROWS = 320
WIDTH = 2048
CUT = 256
GRID_COLS = 8
TILES = 256
PLANES = 2
HALF = 144
EAST_HALF = 176
MESH = pl.DeviceIdType.MESH
F32 = jnp.float32
U_ROWS, U_COLS, U_TURN = 8, 4, 1
BF16 = jnp.bfloat16


def two_parts(table):
    high = table.astype(ml_dtypes.bfloat16)
    low = (table - high.astype(np.float64)).astype(ml_dtypes.bfloat16)
    return high, low


def three_parts(table):
    parts = []
    for _ in range(3):
        parts.append(table.astype(ml_dtypes.bfloat16))
        table = table - parts[-1].astype(table.dtype)
    return parts


def angles(rows, cols, length):
    product = np.outer(np.arange(rows), np.arange(cols)) % length
    return product * (2.0 * np.pi / length)


def row_tables(length, cols):
    count = length // 2 + 1
    turn = angles(count, length, length)
    weight = np.full((count, 1), 2.0)
    weight[0] = weight[-1] = 1.0
    scale = 1.0 / math.sqrt(length * cols)
    forward = np.cos(turn), -np.sin(turn)
    backward = (weight * np.cos(turn)).T * scale, (weight * np.sin(turn)).T * scale
    return forward, backward


AT_ROWS, AT_BACK, AT_EAST_ROWS, AT_EAST_BACK, AT_COLS, AT_TWIST, BUNDLE = 0, 256, 512, 864, 1184, 1696, 1728


def bundle():
    out = np.zeros((BUNDLE, 768), ml_dtypes.bfloat16)

    def put(row, col, table):
        out[row : row + table.shape[0], col : col + table.shape[1]] = table

    (cos, sin), (back_cos, back_sin) = row_tables(CUT, WIDTH)
    high, low = two_parts(np.concatenate([cos, sin[1:-1]]))
    put(AT_ROWS, 0, np.concatenate([high, high, low], axis=1))
    high, low = two_parts(np.concatenate([back_cos, back_sin[:, 1:-1]], axis=1))
    put(AT_BACK, 0, np.concatenate([high, high, low], axis=1))
    (cos, sin), (back_cos, back_sin) = row_tables(ROWS, CUT)
    whole = np.zeros((2 * EAST_HALF, ROWS))
    whole[: len(cos)], whole[EAST_HALF : EAST_HALF + len(sin)] = cos, sin
    for i, part in enumerate(two_parts(whole)):
        put(AT_EAST_ROWS, 384 * i, part)
    whole = np.zeros((ROWS, 2 * EAST_HALF))
    whole[:, : len(cos)], whole[:, EAST_HALF : EAST_HALF + len(sin)] = back_cos, back_sin
    for i, part in enumerate(two_parts(whole)):
        put(AT_EAST_BACK, 384 * i, part)
    turn = angles(CUT, CUT, CUT)
    for i, part in enumerate(two_parts(np.concatenate([np.cos(turn), np.sin(turn)], axis=1))):
        put(AT_COLS + CUT * i, 0, part)
    turn = angles(128, 128, 128)
    cos, sin = np.cos(turn), np.sin(turn)
    for i, part in enumerate(two_parts(np.block([[cos, -sin], [sin, cos]]))):
        put(AT_COLS + CUT * i, 512, part)
    turn = angles(16, 128, WIDTH)
    for i, part in enumerate(three_parts(np.concatenate([np.cos(turn), -np.sin(turn)]).astype(np.float32))):
        put(AT_TWIST, 128 * i, part)
    return out


def table_rows3(t):
    return t[AT_ROWS : AT_ROWS + 256, :]


def table_back3(t):
    return t[AT_BACK : AT_BACK + 256, :]


def table_cols3(t):
    high = t[AT_COLS : AT_COLS + 256, 512:]
    return jnp.concatenate([high, high, t[AT_COLS + 256 : AT_COLS + 512, 512:]], axis=0)


def table_twist(t):
    parts = [t[AT_TWIST : AT_TWIST + 32, 128 * i : 128 * i + 128].astype(F32) for i in range(3)]
    return (parts[0] + parts[1]) + parts[2]


def pair_of(t, row, rows, cols):
    return t[row : row + rows, :cols], t[row : row + rows, 384 : 384 + cols]


def dot(a, b):
    return jnp.dot(a, b, preferred_element_type=F32)


def three(x, axis):
    high, low = split(x)
    return jnp.concatenate([high, low, high], axis=axis)


def split(x):
    high = x.astype(BF16)
    return high, (x - high.astype(F32)).astype(BF16)


def left_dot(table, x):
    high, low = split(x)
    return dot(table[0], high) + (dot(table[0], low) + dot(table[1], high))


def right_dot(x, table):
    high, low = split(x)
    return dot(high, table[0]) + (dot(low, table[0]) + dot(high, table[1]))


def butterfly(re, im):
    size = len(re)
    if size == 1:
        return re, im
    even_re, even_im = butterfly(re[::2], im[::2])
    odd_re, odd_im = butterfly(re[1::2], im[1::2])
    top_re, top_im, low_re, low_im = [], [], [], []
    root = math.sqrt(0.5)
    for k in range(size // 2):
        a, b = odd_re[k], odd_im[k]
        if k == 0:
            pass
        elif 4 * k == size:
            a, b = b, -a
        elif 8 * k == size:
            a, b = root * (a + b), root * (b - a)
        elif 8 * k == 3 * size:
            a, b = root * (b - a), -root * (a + b)
        else:
            c, s = math.cos(2 * math.pi * k / size), math.sin(2 * math.pi * k / size)
            a, b = c * a + s * b, c * b - s * a
        top_re.append(even_re[k] + a)
        top_im.append(even_im[k] + b)
        low_re.append(even_re[k] - a)
        low_im.append(even_im[k] - b)
    return top_re + low_re, top_im + low_im


def at(start, size, step):
    return pl.ds(pl.multiple_of(start, step), size)


def loop(count, f, at_once=1):
    def step(i, c):
        for j in range(at_once):
            f(i * at_once + j)
        return c

    lax.fori_loop(0, count // at_once, step, 0)


def moved(x, steps, axis):
    count = jnp.full(x.shape, steps, jnp.int32)
    for bit in (32, 16, 8, 4, 2, 1):
        x = jnp.where((count & bit) != 0, pltpu.roll(x, bit, axis), x)
    return x


def fold(to, whole, offset, factor=None):
    def scaled(x):
        return x if factor is None else x * factor

    start = ROWS - CUT - offset

    def low(i):
        r = at(i * 8, 8, 8)
        rest = jnp.full((8, 512), start - i * 8, jnp.int32)
        late = lax.broadcasted_iota(jnp.int32, (8, 512), 0) < rest
        for c in range(0, WIDTH, 512):
            cols = slice(c, c + 512)
            to[r, cols] = scaled(jnp.where(late, whole[at(CUT + i * 8, 8, 8), cols], whole[r, cols]))

    def high(i):
        r = at(ROWS - CUT + i * 8, 8, 8)
        to[r, :] = scaled(whole[r, :])

    loop((ROWS - CUT) // 8, low)
    loop((2 * CUT - ROWS) // 8, high)


def south_forward(strip_of, t, twist, y, z, spec):
    twist[...] = table_twist(t)
    for r in (128, HALF + 128):
        y[r : r + 16, :] = jnp.zeros((16, WIDTH), F32)
    top = lax.broadcasted_iota(jnp.int32, (8, 256), 0) == 0

    def rows_step(i):
        cols = at(i * 256, 256, 256)
        d = dot(table_rows3(t), three(strip_of(cols), 0))
        y[:128, cols] = d[:128]
        y[128:136, cols] = jnp.where(top, d[128:136], 0.0)
        y[HALF : HALF + 8, cols] = jnp.where(top, 0.0, d[128:136])
        y[HALF + 8 : HALF + 128, cols] = d[136:]

    loop(8, rows_step, U_ROWS)

    def turn_step(i):
        top, low = at(i * 8, 8, 8), at(HALF + i * 8, 8, 8)
        re = [y[top, 128 * a : 128 * a + 128] for a in range(16)]
        im = [y[low, 128 * a : 128 * a + 128] for a in range(16)]
        re, im = butterfly(re, im)
        for k in range(16):
            c, s = twist[k : k + 1, :], twist[16 + k : 17 + k, :]
            to = at(k * HALF + i * 8, 8, 8)
            z[to, :128] = re[k] * c - im[k] * s
            z[to, 128:] = re[k] * s + im[k] * c

    loop(HALF // 8, turn_step, U_TURN)

    def cols_step(i):
        to = at(i * 576, 576, 8)
        spec[to, :] = dot(three(z[to, :], 1), table_cols3(t))

    loop(4, cols_step, U_COLS)


def half_weight(first, rows, last):
    h = first + lax.broadcasted_iota(jnp.int32, (rows, 128), 0)
    return jnp.where(h < last, jnp.where(h == 0, 1.0, 2.0), jnp.where(h == last, 1.0, 0.0))


def south_kernel(offsets, own, ready, east, strip, inv, dark, t, corrected, east_out, out, y, z, spec, mag, twist, phase, sems):
    writes = [pltpu.make_async_copy(ready, corrected, sems.at[0]), pltpu.make_async_copy(east, east_out, sems.at[1])]
    for w in writes:
        w.start()

    north = jnp.maximum(lax.axis_index("gz") * lax.axis_size("ta") + lax.axis_index("ta") - GRID_COLS, 0)
    start = ROWS - CUT - offsets[1, north]
    angle = (lax.broadcasted_iota(jnp.int32, (HALF, 128), 0) * start & (CUT - 1)).astype(F32) * (2.0 * math.pi / CUT)
    phase[0], phase[1] = jnp.cos(angle), jnp.sin(angle)

    def strip_of(cols):
        return (0.5 * strip[:, cols] - dark[:, cols]) * inv[:, cols]

    south_forward(strip_of, t, twist, y, z, spec)

    def cross_step(i, total):
        part = jnp.zeros((8, 128), F32)
        for k in range(16):
            here = at(k * HALF + i * 8, 8, 8)
            ar, ai = own[here, :128], own[here, 128:]
            br, bi = spec[here, :128], spec[here, 128:]
            cr = ar * br + ai * bi
            ci = ai * br - ar * bi
            size = jnp.sqrt(cr * cr + ci * ci)
            z[here, :128] = cr
            z[here, 128:] = -ci
            mag[here, :] = size
            part = part + size
        return total + part * half_weight(i * 8, 8, CUT // 2)

    total = lax.fori_loop(0, HALF // 8, cross_step, jnp.zeros((8, 128), F32))
    floor = jnp.sum(total) * (1.0 / (CUT * WIDTH)) + 1e-06

    def cols_step(i):
        here = at(i * 288, 288, 8)
        scale = 1.0 / (mag[here, :] + floor)
        x = jnp.concatenate([z[here, :128] * scale, z[here, 128:] * scale], axis=1)
        spec[here, :] = dot(three(x, 1), table_cols3(t))

    loop(8, cols_step, 2 * U_COLS)

    def turn_step(i):
        re, im = [], []
        for k in range(16):
            c, s = twist[k : k + 1, :], twist[16 + k : 17 + k, :]
            here = at(k * HALF + i * 8, 8, 8)
            a, b = spec[here, :128], spec[here, 128:]
            re.append(a * c - b * s)
            im.append(a * s + b * c)
        re, im = butterfly(re, im)
        top, low = at(i * 8, 8, 8), at(HALF + i * 8, 8, 8)
        c, s = phase[0, top, :], phase[1, top, :]
        for a in range(16):
            y[top, 128 * a : 128 * a + 128] = re[a] * c - im[a] * s
            y[low, 128 * a : 128 * a + 128] = re[a] * s + im[a] * c

    loop(HALF // 8, turn_step, U_TURN)

    top = lax.broadcasted_iota(jnp.int32, (8, 256), 0) == 0

    def rows_step(i):
        cols = at(i * 256, 256, 256)
        nyquist = y[128:136, cols]
        first = jnp.where(top, nyquist, y[HALF : HALF + 8, cols])
        x = jnp.concatenate([y[:128, cols], first, y[HALF + 8 : HALF + 128, cols]], axis=0)
        out[:, cols] = dot(table_back3(t), three(x, 0))

    loop(8, rows_step, U_ROWS)
    for w in writes:
        w.wait()


def east_into(out, x, t):
    half = EAST_HALF
    y = left_dot(pair_of(t, AT_EAST_ROWS, 2 * half, ROWS), x)
    cols = t[AT_COLS : AT_COLS + CUT, :512], t[AT_COLS + CUT : AT_COLS + 2 * CUT, :512]

    def columns(v):
        p = right_dot(v, cols)
        return p[:half, :CUT] + p[half:, CUT:], p[half:, :CUT] - p[:half, CUT:]

    ar, ai = columns(y[:, :CUT])
    br, bi = columns(y[:, CUT:])
    cr = ar * br + ai * bi
    ci = ai * br - ar * bi
    size = jnp.sqrt(cr * cr + ci * ci)
    weighted = (size[:, :128] + size[:, 128:]) * half_weight(0, half, ROWS // 2)
    floor = jnp.sum(weighted) * (1.0 / (ROWS * CUT)) + 1e-06
    scale = 1.0 / (size + floor)
    vr, vi = columns(jnp.concatenate([cr * scale, -ci * scale], axis=0))
    out[...] = left_dot(pair_of(t, AT_EAST_BACK, ROWS, 2 * half), jnp.concatenate([vr, vi], axis=0))


CHAINS = 4
BAND = ROWS // CHAINS
RING = 8
BLOCK = ROWS // RING
WIDTHS = (1024, 512, 256, 128)
REACH = 3


def first_kernel(
    offsets, raw, bundled,
    tile, strip, spec, east, inv_south, dark_south, t,
    out, sums, west, mine, logs, acc, first, recv1, recv2, recv3, recv4, near, far, hop, spec_y, spec_z, both, twist,
    load, send, recv,
):
    gz, ta = lax.axis_index("gz"), lax.axis_index("ta")
    y, z = gz // 2, (ta // 8) * 2 + gz % 2
    x, core = (ta // 2) % 4, ta % 2
    other = 1 - core

    loads = []
    for q in range(CHAINS):
        band = pl.ds(q * BAND, BAND)
        c = pltpu.make_async_copy(raw.at[:, band], tile.at[:, band], load.at[q])
        c.start()
        loads.append(c)

    table_load = pltpu.make_async_copy(bundled, t, load.at[CHAINS])
    table_load.start()

    def device(x, y, z, core):
        z = (z + RING) % RING
        return (y * 2 + z % 2, (z // 2) * 8 + x * 2 + core)

    def beside(p):
        return p + 1 - 2 * (p % 2)

    def across(p):
        return 3 - p

    def gray(p):
        return (p + p // 2) % 2

    def upper(p):
        return p // 2

    def along(axis, move):
        on_x = (1 - core) if axis == 0 else core
        return device(x + on_x * (move(x) - x), y + (1 - on_x) * (move(y) - y), z, core)

    place = (x + core * (y - x), y + core * (x - y))
    partner_core = device(x, y, z, other)
    partner = {(axis, move): along(axis, move) for axis in (0, 1) for move in (beside, across)}
    down = [device(x, y, z - d, core) for d in range(1, REACH + 1)]
    up = [device(x, y, z + d, core) for d in range(1, REACH + 1)]
    count_ta = lax.axis_size("ta")
    before, after = (gz, (ta + count_ta - 1) % count_ta), (gz, (ta + 1) % count_ta)

    south = (gz, (ta + GRID_COLS) % count_ta)
    north = (gz, (ta + count_ta - GRID_COLS) % count_ta)
    has_south, has_north = ta < count_ta - GRID_COLS, ta >= GRID_COLS
    own_tile = gz * count_ta + ta

    barrier = pltpu.get_barrier_semaphore()
    everyone = [partner_core, *partner.values(), *down, *up, before, after, south, north]
    for d in everyone:
        pl.semaphore_signal(barrier, inc=1, device_id=d, device_id_type=MESH)

    count = [0]
    started = []

    def copy(src, dst, to):
        i = count[0]
        count[0] += 1
        c = pltpu.make_async_remote_copy(
            src_ref=src, dst_ref=dst, send_sem=send.at[i], recv_sem=recv.at[i], device_id=to, device_id_type=MESH
        )
        c.start()
        started.append(c)
        return c

    def band(q):
        return pl.ds(q * BAND, BAND)

    for q in range(CHAINS):
        loads[q].wait()

        def add_planes(i, q=q):
            r = at(q * BAND + i * 8, 8, 8)
            sums[r, :] = tile[0, r, :] + tile[1, r, :]

        loop(BAND // 8, add_planes)

    fold(mine, sums, offsets[1, own_tile])
    pl.semaphore_wait(barrier, len(everyone))
    south_copy = pltpu.make_async_remote_copy(
        src_ref=mine, dst_ref=strip, send_sem=send.at[COPIES], recv_sem=recv.at[COPIES], device_id=south, device_id_type=MESH
    )

    @pl.when(has_south)
    def _():
        south_copy.start()

    @pl.when(jnp.logical_not(has_north))
    def _():
        strip[...] = jnp.zeros_like(strip)

    beside_copy = copy(sums.at[:, pl.ds(0, CUT)], west, before)

    orders = [
        [(0, beside, gray), (0, across, upper), (1, beside, gray), (1, across, upper)],
        [(0, across, upper), (0, beside, gray), (1, across, upper), (1, beside, gray)],
    ]
    moves = [orders[q % 2] for q in range(CHAINS)]
    into = [recv1, recv2, recv3, recv4]
    bases = [[0] for q in range(CHAINS)]
    flight = []
    for q in range(CHAINS):

        def take(i, q=q):
            r = at(q * BAND + i * 8, 8, 8)
            for c in range(0, WIDTH, 512):
                cols = slice(c, c + 512)
                one, two = jnp.log(tile[0, r, cols]), jnp.log(tile[1, r, cols])
                logs[0, r, cols] = one + two
                logs[1, r, cols] = jnp.minimum(one, two)

        loop(BAND // 8, take)
        bit = moves[q][0][2](place[1])
        halves = [at((1 - bit) * 1024, 1024, 128), at(bit * 1024, 1024, 128)]
        flight.append([copy(logs.at[other, band(q), c], first.at[band(q), c], partner_core) for c in halves])

    steps = len(WIDTHS)
    for q in range(CHAINS):

        def add_first(i, q=q, c=0):
            r = at(q * BAND + i * 8, 8, 8)
            acc[r, c] = logs[core, r, c] + first[r, c]

        halves = flight[q]
        axis, move, bit = moves[q][0]
        b = bit(place[axis])
        c = at((1 - b) * 1024, 1024, 128)
        halves[0].wait_recv()
        loop(BAND // 8, lambda i, q=q, c=c: add_first(i, q, c))
        flight[q] = copy(acc.at[band(q), c], into[0].at[band(q)], partner[(axis, move)])
        c = at(b * 1024, 1024, 128)
        halves[1].wait_recv()
        loop(BAND // 8, lambda i, q=q, c=c: add_first(i, q, c))
        bases[q].append(b * 1024)
    for step in range(1, steps + 1):
        for q in range(CHAINS):
            flight[q].wait_recv()
            w = WIDTHS[step - 1]

            def add_next(i, q=q, c=at(bases[q][step], w, 128), buf=into[step - 1]):
                r = at(q * BAND + i * 8, 8, 8)
                acc[r, c] = acc[r, c] + buf[r, :]

            loop(BAND // 8, add_next)
            if step < steps:
                axis, move, bit = moves[q][step]
                w = WIDTHS[step]
                b = bit(place[axis])
                base = bases[q][step]
                flight[q] = copy(
                    acc.at[band(q), at(base + (1 - b) * w, w, 128)], into[step].at[band(q)], partner[(axis, move)]
                )
                bases[q].append(base + b * w)

    def block(shift):
        j = (z + shift + RING) % RING
        col = bases[0][steps] + ((j // 2) % 2) * (bases[1][steps] - bases[0][steps])
        return at(j * BLOCK, BLOCK, 8), at(col, 128, 128)

    fars, nears = [], []
    for d in range(1, REACH + 1):
        r, c = block(4 - d)
        fars.append(copy(acc.at[r, c], far.at[d - 1], down[d - 1]))
    for d in range(1, REACH + 1):
        r, c = block(-d)
        nears.append(copy(acc.at[r, c], near.at[d - 1], down[d - 1]))
    for f in fars:
        f.wait_recv()
    r, c = block(4)
    acc[r, c] = (acc[r, c] + far[0]) + (far[1] + far[2])
    f = copy(acc.at[r, c], hop.at[0], down[2])
    f.wait_recv()
    f = copy(hop.at[0], hop.at[1], down[0])
    for n in nears:
        n.wait_recv()
    r, c = block(0)
    total = (acc[r, c] + near[0]) + (near[1] + near[2])
    f.wait_recv()
    total = total + hop[1]
    is_floor = core.astype(F32)
    scale = is_floor * (1.0 / TILES) - (1.0 - is_floor) * (1.0 / (TILES * PLANES))
    out[core, r, c] = (1.0 - 0.5 * is_floor) * jnp.exp(total * scale)

    def give(r, c, to):
        return copy(out.at[core, r, c], out.at[core, r, c], to)

    ones = [give(*block(0), to) for to in down]
    ones[0].wait_recv()
    f = give(*block(1), down[2])
    f.wait_recv()
    fours = [give(*block(4), to) for to in down]
    for f in ones[1:] + fours:
        f.wait_recv()
    passed = []

    def pass_on(q, base, w):
        passed.append(give(band(q), at(base, w, 128), partner_core))

    for step in range(steps - 1, -1, -1):
        for q in range(CHAINS):
            w = WIDTHS[step]
            if step < steps - 1:
                flight[q].wait_recv()
            axis, move, _ = moves[q][step]
            flight[q] = give(band(q), at(bases[q][step + 1], w, 128), partner[(axis, move)])
            if step == steps - 1:
                pass_on(q, bases[q][steps], w)
            else:
                pass_on(q, 2 * bases[q][step + 1] + WIDTHS[step + 1] - bases[q][step + 2], WIDTHS[step + 1])
    for q in range(CHAINS):
        flight[q].wait_recv()
        pass_on(q, WIDTHS[0] - bases[q][1], WIDTHS[0])
    for c in passed:
        c.wait_recv()
    beside_copy.wait_recv()

    table_load.wait()

    def own_of(cols):
        return (0.5 * sums[:CUT, cols] - out[1, :CUT, cols]) * out[0, :CUT, cols]

    south_forward(own_of, t, twist, spec_y, spec_z, spec)
    has_east = (ta < count_ta - 1).astype(F32)

    def strips(i):
        r, last = at(i * 64, 64, 64), slice(WIDTH - 3 * 128, WIDTH)
        eastern = (0.5 * sums[r, last] - out[1, r, last]) * out[0, r, last]
        both[r, :CUT] = moved(eastern, offsets[0, own_tile], 1)[:, 128:]
        both[r, CUT:] = (0.5 * west[r, :] - out[1, r, :CUT]) * out[0, r, :CUT] * has_east

    loop(ROWS // 64, strips)
    east_into(east, both[...], t)

    def correct(i):
        r = at(i * 8, 8, 8)
        for c in range(0, WIDTH, 512):
            cols = slice(c, c + 512)
            g, d = out[0, r, cols], out[1, r, cols]
            for p in range(PLANES):
                tile[p, r, cols] = (tile[p, r, cols] - d) * g

    loop(ROWS // 8, correct)
    north_tile = jnp.maximum(own_tile - GRID_COLS, 0)
    north_is = has_north.astype(F32)

    fold(inv_south, out.at[0], offsets[1, north_tile], north_is)
    fold(dark_south, out.at[1], offsets[1, north_tile])

    @pl.when(has_north)
    def _():
        south_copy.wait_recv()

    for c in started:
        c.wait_send()

    @pl.when(has_south)
    def _():
        south_copy.wait_send()


COPIES = CHAINS * (2 * len(WIDTHS) + 2 + len(WIDTHS) + 1) + 1 + (2 * REACH + 2) + (2 * REACH + 1)


VMEM = pl.BlockSpec(memory_space=pltpu.VMEM)
SMEM = pl.BlockSpec(memory_space=pltpu.SMEM)
ANY = pl.BlockSpec(memory_space=pl.ANY)
HBM = pl.BlockSpec(memory_space=pltpu.HBM)
SPEC = (16 * HALF, 256)
FIRST_LIMIT = 34


def shape(*dims):
    return jax.ShapeDtypeStruct(dims, F32)


def body(raw_planes, offsets):
    offsets = offsets.T
    table = jax.ShapeDtypeStruct((BUNDLE, 768), BF16)
    ready, strip, spec, east, inv, dark, tables = pl.pallas_call(
        first_kernel,
        out_shape=(
            shape(PLANES, ROWS, WIDTH), shape(CUT, WIDTH), shape(*SPEC), shape(ROWS, CUT), shape(CUT, WIDTH), shape(CUT, WIDTH), table,
        ),
        in_specs=[SMEM, ANY, ANY],
        out_specs=(VMEM,) * 7,
        scratch_shapes=[
            pltpu.VMEM((2, ROWS, WIDTH), F32),
            pltpu.VMEM((ROWS, WIDTH), F32),
            pltpu.VMEM((ROWS, CUT), F32),
            pltpu.VMEM((CUT, WIDTH), F32),
            pltpu.VMEM((2, ROWS, WIDTH), F32),
            pltpu.VMEM((ROWS, WIDTH), F32),
            pltpu.VMEM((ROWS, WIDTH), F32),
            *[pltpu.VMEM((ROWS, w), F32) for w in WIDTHS],
            pltpu.VMEM((REACH, BLOCK, 128), F32),
            pltpu.VMEM((REACH, BLOCK, 128), F32),
            pltpu.VMEM((2, BLOCK, 128), F32),
            pltpu.VMEM((2 * HALF, WIDTH), F32),
            pltpu.VMEM(SPEC, F32),
            pltpu.VMEM((ROWS, 2 * CUT), F32),
            pltpu.VMEM((32, 128), F32),
            pltpu.SemaphoreType.DMA((CHAINS + 1,)),
            pltpu.SemaphoreType.DMA((COPIES + 1,)),
            pltpu.SemaphoreType.DMA((COPIES + 1,)),
        ],
        compiler_params=pltpu.CompilerParams(collective_id=0, has_side_effects=True, vmem_limit_bytes=FIRST_LIMIT << 20),
        name="first",
    )(offsets, raw_planes[0], bundle())
    corrected, east_corr, south_corr = pl.pallas_call(
        south_kernel,
        out_shape=(shape(PLANES, ROWS, WIDTH), shape(ROWS, CUT), shape(CUT, WIDTH)),
        in_specs=[SMEM] + [VMEM] * 7,
        out_specs=(ANY, ANY, VMEM),
        scratch_shapes=[
            pltpu.VMEM((2 * HALF, WIDTH), F32),
            pltpu.VMEM(SPEC, F32),
            pltpu.VMEM(SPEC, F32),
            pltpu.VMEM((16 * HALF, 128), F32),
            pltpu.VMEM((32, 128), F32),
            pltpu.VMEM((2, HALF, 128), F32),
            pltpu.SemaphoreType.DMA((2,)),
        ],
        compiler_params=pltpu.CompilerParams(vmem_limit_bytes=20 << 20),
        name="second",
    )(offsets, spec, ready, east, strip, inv, dark, tables)
    return (corrected[None], east_corr[None], south_corr[None])


def solution(mesh):
    in_specs = (P(("gz", "ta"), None, None, None), P())
    out_specs = (
        P(("gz", "ta"), None, None, None),
        P(("gz", "ta"), None, None),
        P(("gz", "ta"), None, None),
    )
    return jax.shard_map(body, mesh=mesh, in_specs=in_specs, out_specs=out_specs, check_vma=False)
```

```python
import math

import jax
import jax.numpy as jnp
import ml_dtypes
import numpy as np
from jax import lax
from jax.experimental import pallas as pl
from jax.experimental.pallas import tpu as pltpu
from jax.sharding import PartitionSpec as P

ROWS = 320
WIDTH = 2048
CUT = 256
GRID_COLS = 8
TILES = 256
PLANES = 2
HALF = 144
EAST_HALF = 176
MESH = pl.DeviceIdType.MESH
F32 = jnp.float32
U_ROWS, U_COLS, U_TURN = 8, 4, 1
BF16 = jnp.bfloat16


def two_parts(table):
    high = table.astype(ml_dtypes.bfloat16)
    low = (table - high.astype(np.float64)).astype(ml_dtypes.bfloat16)
    return high, low


def three_parts(table):
    parts = []
    for _ in range(3):
        parts.append(table.astype(ml_dtypes.bfloat16))
        table = table - parts[-1].astype(table.dtype)
    return parts


def angles(rows, cols, length):
    product = np.outer(np.arange(rows), np.arange(cols)) % length
    return product * (2.0 * np.pi / length)


def row_tables(length, cols):
    count = length // 2 + 1
    turn = angles(count, length, length)
    weight = np.full((count, 1), 2.0)
    weight[0] = weight[-1] = 1.0
    scale = 1.0 / math.sqrt(length * cols)
    forward = np.cos(turn), -np.sin(turn)
    backward = (weight * np.cos(turn)).T * scale, (weight * np.sin(turn)).T * scale
    return forward, backward


AT_ROWS, AT_BACK, AT_EAST_ROWS, AT_EAST_BACK, AT_COLS, AT_TWIST, BUNDLE = 0, 256, 512, 864, 1184, 1696, 1728


def bundle():
    out = np.zeros((BUNDLE, 768), ml_dtypes.bfloat16)

    def put(row, col, table):
        out[row : row + table.shape[0], col : col + table.shape[1]] = table

    (cos, sin), (back_cos, back_sin) = row_tables(CUT, WIDTH)
    high, low = two_parts(np.concatenate([cos, sin[1:-1]]))
    put(AT_ROWS, 0, np.concatenate([high, high, low], axis=1))
    high, low = two_parts(np.concatenate([back_cos, back_sin[:, 1:-1]], axis=1))
    put(AT_BACK, 0, np.concatenate([high, high, low], axis=1))
    (cos, sin), (back_cos, back_sin) = row_tables(ROWS, CUT)
    whole = np.zeros((2 * EAST_HALF, ROWS))
    whole[: len(cos)], whole[EAST_HALF : EAST_HALF + len(sin)] = cos, sin
    for i, part in enumerate(two_parts(whole)):
        put(AT_EAST_ROWS, 384 * i, part)
    whole = np.zeros((ROWS, 2 * EAST_HALF))
    whole[:, : len(cos)], whole[:, EAST_HALF : EAST_HALF + len(sin)] = back_cos, back_sin
    for i, part in enumerate(two_parts(whole)):
        put(AT_EAST_BACK, 384 * i, part)
    turn = angles(CUT, CUT, CUT)
    for i, part in enumerate(two_parts(np.concatenate([np.cos(turn), np.sin(turn)], axis=1))):
        put(AT_COLS + CUT * i, 0, part)
    turn = angles(128, 128, 128)
    cos, sin = np.cos(turn), np.sin(turn)
    for i, part in enumerate(two_parts(np.block([[cos, -sin], [sin, cos]]))):
        put(AT_COLS + CUT * i, 512, part)
    turn = angles(16, 128, WIDTH)
    for i, part in enumerate(three_parts(np.concatenate([np.cos(turn), -np.sin(turn)]).astype(np.float32))):
        put(AT_TWIST, 128 * i, part)
    return out


def table_rows3(t):
    return t[AT_ROWS : AT_ROWS + 256, :]


def table_back3(t):
    return t[AT_BACK : AT_BACK + 256, :]


def table_cols3(t):
    high = t[AT_COLS : AT_COLS + 256, 512:]
    return jnp.concatenate([high, high, t[AT_COLS + 256 : AT_COLS + 512, 512:]], axis=0)


def table_twist(t):
    parts = [t[AT_TWIST : AT_TWIST + 32, 128 * i : 128 * i + 128].astype(F32) for i in range(3)]
    return (parts[0] + parts[1]) + parts[2]


def pair_of(t, row, rows, cols):
    return t[row : row + rows, :cols], t[row : row + rows, 384 : 384 + cols]


def dot(a, b):
    return jnp.dot(a, b, preferred_element_type=F32)


def three(x, axis):
    high, low = split(x)
    return jnp.concatenate([high, low, high], axis=axis)


def split(x):
    high = x.astype(BF16)
    return high, (x - high.astype(F32)).astype(BF16)


def left_dot(table, x):
    high, low = split(x)
    return dot(table[0], high) + (dot(table[0], low) + dot(table[1], high))


def right_dot(x, table):
    high, low = split(x)
    return dot(high, table[0]) + (dot(low, table[0]) + dot(high, table[1]))


def butterfly(re, im):
    size = len(re)
    if size == 1:
        return re, im
    even_re, even_im = butterfly(re[::2], im[::2])
    odd_re, odd_im = butterfly(re[1::2], im[1::2])
    top_re, top_im, low_re, low_im = [], [], [], []
    root = math.sqrt(0.5)
    for k in range(size // 2):
        a, b = odd_re[k], odd_im[k]
        if k == 0:
            pass
        elif 4 * k == size:
            a, b = b, -a
        elif 8 * k == size:
            a, b = root * (a + b), root * (b - a)
        elif 8 * k == 3 * size:
            a, b = root * (b - a), -root * (a + b)
        else:
            c, s = math.cos(2 * math.pi * k / size), math.sin(2 * math.pi * k / size)
            a, b = c * a + s * b, c * b - s * a
        top_re.append(even_re[k] + a)
        top_im.append(even_im[k] + b)
        low_re.append(even_re[k] - a)
        low_im.append(even_im[k] - b)
    return top_re + low_re, top_im + low_im


def at(start, size, step):
    return pl.ds(pl.multiple_of(start, step), size)


def loop(count, f, at_once=1):
    def step(i, c):
        for j in range(at_once):
            f(i * at_once + j)
        return c

    lax.fori_loop(0, count // at_once, step, 0)


def moved(x, steps, axis):
    count = jnp.full(x.shape, steps, jnp.int32)
    for bit in (32, 16, 8, 4, 2, 1):
        x = jnp.where((count & bit) != 0, pltpu.roll(x, bit, axis), x)
    return x


def scaled(x, factor):
    return x if factor is None else x * factor


def fold_low(to, whole, offset, factor=None):
    start = ROWS - CUT - offset

    def low(i):
        r = at(i * 8, 8, 8)
        rest = jnp.full((8, 512), start - i * 8, jnp.int32)
        late = lax.broadcasted_iota(jnp.int32, (8, 512), 0) < rest
        for c in range(0, WIDTH, 512):
            cols = slice(c, c + 512)
            to[r, cols] = scaled(jnp.where(late, whole[at(CUT + i * 8, 8, 8), cols], whole[r, cols]), factor)

    loop((ROWS - CUT) // 8, low)


def fold_high(to, whole, first, last, factor=None):
    def high(i):
        r = at(first + i * 8, 8, 8)
        to[r, :] = scaled(whole[r, :], factor)

    loop((last - first) // 8, high)


def fold(to, whole, offset, factor=None):
    fold_low(to, whole, offset, factor)
    fold_high(to, whole, ROWS - CUT, CUT, factor)


def south_forward(strip_of, t, twist, y, z, spec):
    twist[...] = table_twist(t)
    for r in (128, HALF + 128):
        y[r : r + 16, :] = jnp.zeros((16, WIDTH), F32)
    top = lax.broadcasted_iota(jnp.int32, (8, 256), 0) == 0

    def rows_step(i):
        cols = at(i * 256, 256, 256)
        d = dot(table_rows3(t), three(strip_of(cols), 0))
        y[:128, cols] = d[:128]
        y[128:136, cols] = jnp.where(top, d[128:136], 0.0)
        y[HALF : HALF + 8, cols] = jnp.where(top, 0.0, d[128:136])
        y[HALF + 8 : HALF + 128, cols] = d[136:]

    loop(8, rows_step, U_ROWS)

    def turn_step(i):
        top, low = at(i * 8, 8, 8), at(HALF + i * 8, 8, 8)
        re = [y[top, 128 * a : 128 * a + 128] for a in range(16)]
        im = [y[low, 128 * a : 128 * a + 128] for a in range(16)]
        re, im = butterfly(re, im)
        for k in range(16):
            c, s = twist[k : k + 1, :], twist[16 + k : 17 + k, :]
            to = at(k * HALF + i * 8, 8, 8)
            z[to, :128] = re[k] * c - im[k] * s
            z[to, 128:] = re[k] * s + im[k] * c

    loop(HALF // 8, turn_step, U_TURN)

    def cols_step(i):
        to = at(i * 576, 576, 8)
        spec[to, :] = dot(three(z[to, :], 1), table_cols3(t))

    loop(4, cols_step, U_COLS)


def half_weight(first, rows, last):
    h = first + lax.broadcasted_iota(jnp.int32, (rows, 128), 0)
    return jnp.where(h < last, jnp.where(h == 0, 1.0, 2.0), jnp.where(h == last, 1.0, 0.0))


def south_kernel(offsets, own, ready, east, strip, inv, dark, t, corrected, east_out, out, y, z, spec, mag, twist, phase, sems):
    writes = [pltpu.make_async_copy(ready, corrected, sems.at[0]), pltpu.make_async_copy(east, east_out, sems.at[1])]
    for w in writes:
        w.start()

    north = jnp.maximum(lax.axis_index("gz") * lax.axis_size("ta") + lax.axis_index("ta") - GRID_COLS, 0)
    start = ROWS - CUT - offsets[1, north]
    angle = (lax.broadcasted_iota(jnp.int32, (HALF, 128), 0) * start & (CUT - 1)).astype(F32) * (2.0 * math.pi / CUT)
    phase[0], phase[1] = jnp.cos(angle), jnp.sin(angle)

    def strip_of(cols):
        return (0.5 * strip[:, cols] - dark[:, cols]) * inv[:, cols]

    south_forward(strip_of, t, twist, y, z, spec)

    def cross_step(i, total):
        part = jnp.zeros((8, 128), F32)
        for k in range(16):
            here = at(k * HALF + i * 8, 8, 8)
            ar, ai = own[here, :128], own[here, 128:]
            br, bi = spec[here, :128], spec[here, 128:]
            cr = ar * br + ai * bi
            ci = ai * br - ar * bi
            size = jnp.sqrt(cr * cr + ci * ci)
            z[here, :128] = cr
            z[here, 128:] = -ci
            mag[here, :] = size
            part = part + size
        return total + part * half_weight(i * 8, 8, CUT // 2)

    total = lax.fori_loop(0, HALF // 8, cross_step, jnp.zeros((8, 128), F32))
    floor = jnp.sum(total) * (1.0 / (CUT * WIDTH)) + 1e-06

    def cols_step(i):
        here = at(i * 288, 288, 8)
        scale = 1.0 / (mag[here, :] + floor)
        x = jnp.concatenate([z[here, :128] * scale, z[here, 128:] * scale], axis=1)
        spec[here, :] = dot(three(x, 1), table_cols3(t))

    loop(8, cols_step, 2 * U_COLS)

    def turn_step(i):
        re, im = [], []
        for k in range(16):
            c, s = twist[k : k + 1, :], twist[16 + k : 17 + k, :]
            here = at(k * HALF + i * 8, 8, 8)
            a, b = spec[here, :128], spec[here, 128:]
            re.append(a * c - b * s)
            im.append(a * s + b * c)
        re, im = butterfly(re, im)
        top, low = at(i * 8, 8, 8), at(HALF + i * 8, 8, 8)
        c, s = phase[0, top, :], phase[1, top, :]
        for a in range(16):
            y[top, 128 * a : 128 * a + 128] = re[a] * c - im[a] * s
            y[low, 128 * a : 128 * a + 128] = re[a] * s + im[a] * c

    loop(HALF // 8, turn_step, U_TURN)

    top = lax.broadcasted_iota(jnp.int32, (8, 256), 0) == 0

    def rows_step(i):
        cols = at(i * 256, 256, 256)
        nyquist = y[128:136, cols]
        first = jnp.where(top, nyquist, y[HALF : HALF + 8, cols])
        x = jnp.concatenate([y[:128, cols], first, y[HALF + 8 : HALF + 128, cols]], axis=0)
        out[:, cols] = dot(table_back3(t), three(x, 0))

    loop(8, rows_step, U_ROWS)
    for w in writes:
        w.wait()


def east_into(out, x, t):
    half = EAST_HALF
    y = left_dot(pair_of(t, AT_EAST_ROWS, 2 * half, ROWS), x)
    cols = t[AT_COLS : AT_COLS + CUT, :512], t[AT_COLS + CUT : AT_COLS + 2 * CUT, :512]

    def columns(v):
        p = right_dot(v, cols)
        return p[:half, :CUT] + p[half:, CUT:], p[half:, :CUT] - p[:half, CUT:]

    ar, ai = columns(y[:, :CUT])
    br, bi = columns(y[:, CUT:])
    cr = ar * br + ai * bi
    ci = ai * br - ar * bi
    size = jnp.sqrt(cr * cr + ci * ci)
    weighted = (size[:, :128] + size[:, 128:]) * half_weight(0, half, ROWS // 2)
    floor = jnp.sum(weighted) * (1.0 / (ROWS * CUT)) + 1e-06
    scale = 1.0 / (size + floor)
    vr, vi = columns(jnp.concatenate([cr * scale, -ci * scale], axis=0))
    out[...] = left_dot(pair_of(t, AT_EAST_BACK, ROWS, 2 * half), jnp.concatenate([vr, vi], axis=0))


CHAINS = 4
BAND = ROWS // CHAINS
RING = 8
BLOCK = ROWS // RING
WIDTHS = (1024, 512, 256, 128)
REACH = 3


def first_kernel(
    offsets, raw, bundled,
    tile, strip, spec, east, inv_south, dark_south, t,
    out, sums, west, mine, logs, acc, first, recv1, recv2, recv3, recv4, near, far, hop, spec_y, spec_z, both, twist,
    load, send, recv,
):
    gz, ta = lax.axis_index("gz"), lax.axis_index("ta")
    y, z = gz // 2, (ta // 8) * 2 + gz % 2
    x, core = (ta // 2) % 4, ta % 2
    other = 1 - core

    loads = []
    for q in range(CHAINS):
        band = pl.ds(q * BAND, BAND)
        c = pltpu.make_async_copy(raw.at[:, band], tile.at[:, band], load.at[q])
        c.start()
        loads.append(c)

    table_load = pltpu.make_async_copy(bundled, t, load.at[CHAINS])
    table_load.start()

    def device(x, y, z, core):
        z = (z + RING) % RING
        return (y * 2 + z % 2, (z // 2) * 8 + x * 2 + core)

    def beside(p):
        return p + 1 - 2 * (p % 2)

    def across(p):
        return 3 - p

    def gray(p):
        return (p + p // 2) % 2

    def upper(p):
        return p // 2

    def along(axis, move):
        on_x = (1 - core) if axis == 0 else core
        return device(x + on_x * (move(x) - x), y + (1 - on_x) * (move(y) - y), z, core)

    place = (x + core * (y - x), y + core * (x - y))
    partner_core = device(x, y, z, other)
    partner = {(axis, move): along(axis, move) for axis in (0, 1) for move in (beside, across)}
    down = [device(x, y, z - d, core) for d in range(1, REACH + 1)]
    up = [device(x, y, z + d, core) for d in range(1, REACH + 1)]
    count_ta = lax.axis_size("ta")
    before, after = (gz, (ta + count_ta - 1) % count_ta), (gz, (ta + 1) % count_ta)

    south = (gz, (ta + GRID_COLS) % count_ta)
    north = (gz, (ta + count_ta - GRID_COLS) % count_ta)
    has_south, has_north = ta < count_ta - GRID_COLS, ta >= GRID_COLS
    own_tile = gz * count_ta + ta

    barrier = pltpu.get_barrier_semaphore()
    everyone = [partner_core, *partner.values(), *down, *up, before, after, south, north]
    for d in everyone:
        pl.semaphore_signal(barrier, inc=1, device_id=d, device_id_type=MESH)

    count = [0]
    started = []

    def copy(src, dst, to):
        i = count[0]
        count[0] += 1
        c = pltpu.make_async_remote_copy(
            src_ref=src, dst_ref=dst, send_sem=send.at[i], recv_sem=recv.at[i], device_id=to, device_id_type=MESH
        )
        c.start()
        started.append(c)
        return c

    def band(q):
        return pl.ds(q * BAND, BAND)

    pieces = [pl.ds(ROWS - CUT, 2 * BAND - (ROWS - CUT)), pl.ds(2 * BAND, CUT - 2 * BAND), pl.ds(0, ROWS - CUT)]
    south_copies = [
        pltpu.make_async_remote_copy(
            src_ref=mine.at[p], dst_ref=strip.at[p], send_sem=send.at[COPIES + i], recv_sem=recv.at[COPIES + i],
            device_id=south, device_id_type=MESH,
        )
        for i, p in enumerate(pieces)
    ]
    for q in range(CHAINS):
        loads[q].wait()

        def add_planes(i, q=q):
            r = at(q * BAND + i * 8, 8, 8)
            sums[r, :] = tile[0, r, :] + tile[1, r, :]

        loop(BAND // 8, add_planes)
        if q == 1:
            fold_high(mine, sums, ROWS - CUT, 2 * BAND)
            pl.semaphore_wait(barrier, len(everyone))

            @pl.when(has_south)
            def _():
                south_copies[0].start()

    fold_high(mine, sums, 2 * BAND, CUT)
    fold_low(mine, sums, offsets[1, own_tile])

    @pl.when(has_south)
    def _():
        for c in south_copies[1:]:
            c.start()

    @pl.when(jnp.logical_not(has_north))
    def _():
        strip[...] = jnp.zeros_like(strip)

    beside_copy = copy(sums.at[:, pl.ds(0, CUT)], west, before)

    orders = [
        [(0, beside, gray), (0, across, upper), (1, beside, gray), (1, across, upper)],
        [(0, across, upper), (0, beside, gray), (1, across, upper), (1, beside, gray)],
    ]
    moves = [orders[q % 2] for q in range(CHAINS)]
    into = [recv1, recv2, recv3, recv4]
    bases = [[0] for q in range(CHAINS)]
    flight = []
    for q in range(CHAINS):

        def take(i, q=q):
            r = at(q * BAND + i * 8, 8, 8)
            for c in range(0, WIDTH, 512):
                cols = slice(c, c + 512)
                one, two = jnp.log(tile[0, r, cols]), jnp.log(tile[1, r, cols])
                logs[0, r, cols] = one + two
                logs[1, r, cols] = jnp.minimum(one, two)

        loop(BAND // 8, take)
        bit = moves[q][0][2](place[1])
        halves = [at((1 - bit) * 1024, 1024, 128), at(bit * 1024, 1024, 128)]
        flight.append([copy(logs.at[other, band(q), c], first.at[band(q), c], partner_core) for c in halves])

    steps = len(WIDTHS)
    for q in range(CHAINS):

        def add_first(i, q=q, c=0):
            r = at(q * BAND + i * 8, 8, 8)
            acc[r, c] = logs[core, r, c] + first[r, c]

        halves = flight[q]
        axis, move, bit = moves[q][0]
        b = bit(place[axis])
        c = at((1 - b) * 1024, 1024, 128)
        halves[0].wait_recv()
        loop(BAND // 8, lambda i, q=q, c=c: add_first(i, q, c))
        flight[q] = copy(acc.at[band(q), c], into[0].at[band(q)], partner[(axis, move)])
        c = at(b * 1024, 1024, 128)
        halves[1].wait_recv()
        loop(BAND // 8, lambda i, q=q, c=c: add_first(i, q, c))
        bases[q].append(b * 1024)
    for step in range(1, steps + 1):
        for q in range(CHAINS):
            flight[q].wait_recv()
            w = WIDTHS[step - 1]

            def add_next(i, q=q, c=at(bases[q][step], w, 128), buf=into[step - 1]):
                r = at(q * BAND + i * 8, 8, 8)
                acc[r, c] = acc[r, c] + buf[r, :]

            loop(BAND // 8, add_next)
            if step < steps:
                axis, move, bit = moves[q][step]
                w = WIDTHS[step]
                b = bit(place[axis])
                base = bases[q][step]
                flight[q] = copy(
                    acc.at[band(q), at(base + (1 - b) * w, w, 128)], into[step].at[band(q)], partner[(axis, move)]
                )
                bases[q].append(base + b * w)

    def block(shift):
        j = (z + shift + RING) % RING
        col = bases[0][steps] + ((j // 2) % 2) * (bases[1][steps] - bases[0][steps])
        return at(j * BLOCK, BLOCK, 8), at(col, 128, 128)

    fars, nears = [], []
    for d in range(1, REACH + 1):
        r, c = block(4 - d)
        fars.append(copy(acc.at[r, c], far.at[d - 1], down[d - 1]))
    for d in range(1, REACH + 1):
        r, c = block(-d)
        nears.append(copy(acc.at[r, c], near.at[d - 1], down[d - 1]))
    for f in fars:
        f.wait_recv()
    r, c = block(4)
    acc[r, c] = (acc[r, c] + far[0]) + (far[1] + far[2])
    f = copy(acc.at[r, c], hop.at[0], down[2])
    f.wait_recv()
    f = copy(hop.at[0], hop.at[1], down[0])
    for n in nears:
        n.wait_recv()
    r, c = block(0)
    total = (acc[r, c] + near[0]) + (near[1] + near[2])
    f.wait_recv()
    total = total + hop[1]
    is_floor = core.astype(F32)
    scale = is_floor * (1.0 / TILES) - (1.0 - is_floor) * (1.0 / (TILES * PLANES))
    out[core, r, c] = (1.0 - 0.5 * is_floor) * jnp.exp(total * scale)

    def give(r, c, to):
        return copy(out.at[core, r, c], out.at[core, r, c], to)

    ones = [give(*block(0), to) for to in down]
    ones[0].wait_recv()
    f = give(*block(1), down[2])
    f.wait_recv()
    fours = [give(*block(4), to) for to in down]
    for f in ones[1:] + fours:
        f.wait_recv()
    passed = []

    def pass_on(q, base, w):
        passed.append(give(band(q), at(base, w, 128), partner_core))

    for step in range(steps - 1, -1, -1):
        for q in range(CHAINS):
            w = WIDTHS[step]
            if step < steps - 1:
                flight[q].wait_recv()
            axis, move, _ = moves[q][step]
            flight[q] = give(band(q), at(bases[q][step + 1], w, 128), partner[(axis, move)])
            if step == steps - 1:
                pass_on(q, bases[q][steps], w)
            else:
                pass_on(q, 2 * bases[q][step + 1] + WIDTHS[step + 1] - bases[q][step + 2], WIDTHS[step + 1])
    for q in range(CHAINS):
        flight[q].wait_recv()
        pass_on(q, WIDTHS[0] - bases[q][1], WIDTHS[0])
    for c in passed:
        c.wait_recv()
    beside_copy.wait_recv()

    table_load.wait()

    def own_of(cols):
        return (0.5 * sums[:CUT, cols] - out[1, :CUT, cols]) * out[0, :CUT, cols]

    south_forward(own_of, t, twist, spec_y, spec_z, spec)
    has_east = (ta < count_ta - 1).astype(F32)

    def strips(i):
        r, last = at(i * 64, 64, 64), slice(WIDTH - 3 * 128, WIDTH)
        eastern = (0.5 * sums[r, last] - out[1, r, last]) * out[0, r, last]
        both[r, :CUT] = moved(eastern, offsets[0, own_tile], 1)[:, 128:]
        both[r, CUT:] = (0.5 * west[r, :] - out[1, r, :CUT]) * out[0, r, :CUT] * has_east

    loop(ROWS // 64, strips)
    east_into(east, both[...], t)

    def correct(i):
        r = at(i * 8, 8, 8)
        for c in range(0, WIDTH, 512):
            cols = slice(c, c + 512)
            g, d = out[0, r, cols], out[1, r, cols]
            for p in range(PLANES):
                tile[p, r, cols] = (tile[p, r, cols] - d) * g

    loop(ROWS // 8, correct)
    north_tile = jnp.maximum(own_tile - GRID_COLS, 0)
    north_is = has_north.astype(F32)

    fold(inv_south, out.at[0], offsets[1, north_tile], north_is)
    fold(dark_south, out.at[1], offsets[1, north_tile])

    @pl.when(has_north)
    def _():
        for c in south_copies:
            c.wait_recv()

    for c in started:
        c.wait_send()

    @pl.when(has_south)
    def _():
        for c in south_copies:
            c.wait_send()


COPIES = CHAINS * (2 * len(WIDTHS) + 2 + len(WIDTHS) + 1) + 1 + (2 * REACH + 2) + (2 * REACH + 1)


VMEM = pl.BlockSpec(memory_space=pltpu.VMEM)
SMEM = pl.BlockSpec(memory_space=pltpu.SMEM)
ANY = pl.BlockSpec(memory_space=pl.ANY)
HBM = pl.BlockSpec(memory_space=pltpu.HBM)
SPEC = (16 * HALF, 256)
FIRST_LIMIT = 34


def shape(*dims):
    return jax.ShapeDtypeStruct(dims, F32)


def body(raw_planes, offsets):
    offsets = offsets.T
    table = jax.ShapeDtypeStruct((BUNDLE, 768), BF16)
    ready, strip, spec, east, inv, dark, tables = pl.pallas_call(
        first_kernel,
        out_shape=(
            shape(PLANES, ROWS, WIDTH), shape(CUT, WIDTH), shape(*SPEC), shape(ROWS, CUT), shape(CUT, WIDTH), shape(CUT, WIDTH), table,
        ),
        in_specs=[SMEM, ANY, ANY],
        out_specs=(VMEM,) * 7,
        scratch_shapes=[
            pltpu.VMEM((2, ROWS, WIDTH), F32),
            pltpu.VMEM((ROWS, WIDTH), F32),
            pltpu.VMEM((ROWS, CUT), F32),
            pltpu.VMEM((CUT, WIDTH), F32),
            pltpu.VMEM((2, ROWS, WIDTH), F32),
            pltpu.VMEM((ROWS, WIDTH), F32),
            pltpu.VMEM((ROWS, WIDTH), F32),
            *[pltpu.VMEM((ROWS, w), F32) for w in WIDTHS],
            pltpu.VMEM((REACH, BLOCK, 128), F32),
            pltpu.VMEM((REACH, BLOCK, 128), F32),
            pltpu.VMEM((2, BLOCK, 128), F32),
            pltpu.VMEM((2 * HALF, WIDTH), F32),
            pltpu.VMEM(SPEC, F32),
            pltpu.VMEM((ROWS, 2 * CUT), F32),
            pltpu.VMEM((32, 128), F32),
            pltpu.SemaphoreType.DMA((CHAINS + 1,)),
            pltpu.SemaphoreType.DMA((COPIES + 3,)),
            pltpu.SemaphoreType.DMA((COPIES + 3,)),
        ],
        compiler_params=pltpu.CompilerParams(collective_id=0, has_side_effects=True, vmem_limit_bytes=FIRST_LIMIT << 20),
        name="first",
    )(offsets, raw_planes[0], bundle())
    corrected, east_corr, south_corr = pl.pallas_call(
        south_kernel,
        out_shape=(shape(PLANES, ROWS, WIDTH), shape(ROWS, CUT), shape(CUT, WIDTH)),
        in_specs=[SMEM] + [VMEM] * 7,
        out_specs=(ANY, ANY, VMEM),
        scratch_shapes=[
            pltpu.VMEM((2 * HALF, WIDTH), F32),
            pltpu.VMEM(SPEC, F32),
            pltpu.VMEM(SPEC, F32),
            pltpu.VMEM((16 * HALF, 128), F32),
            pltpu.VMEM((32, 128), F32),
            pltpu.VMEM((2, HALF, 128), F32),
            pltpu.SemaphoreType.DMA((2,)),
        ],
        compiler_params=pltpu.CompilerParams(vmem_limit_bytes=20 << 20),
        name="second",
    )(offsets, spec, ready, east, strip, inv, dark, tables)
    return (corrected[None], east_corr[None], south_corr[None])


def solution(mesh):
    in_specs = (P(("gz", "ta"), None, None, None), P())
    out_specs = (
        P(("gz", "ta"), None, None, None),
        P(("gz", "ta"), None, None),
        P(("gz", "ta"), None, None),
    )
    return jax.shard_map(body, mesh=mesh, in_specs=in_specs, out_specs=out_specs, check_vma=False)
```
